128 devices in a mesh: ty: 8 (over z, core), tx: 16 (over x, y).
Axes of the slice: x: 4, y: 4, z: 4, core: 2. Of those that a mesh axis runs over, the one named last changes fastest.
Arguments:
- spectra: float32 [36, 36, 32, 2048], P(None, None, 'ty', 'tx'), may hold values from 0.05 to 2
- sea_mask: int32 [32, 2048], P('ty', 'tx'), may hold values from 0 to 1, as said below
- currents: float32 [2, 131072], P(None, ('ty', 'tx')), may hold values from -3.6 to 3.6
- sea_depth: float32 [131072], P(('ty', 'tx')), may hold values from 10 to 4000
- slopes: float32 [2, 131072], P(None, ('ty', 'tx')), may hold values from -0.018 to 0.018
- piece_offset: int32 [128, 128], replicated, may hold values from 0 to 1020, as said below
- piece_count: int32 [128, 128], replicated, may hold values from 0 to 4, as said below
Outputs:
- advanced: float32 [36, 36, 32, 2048], P(None, None, 'ty', 'tx')
The draws below stay inside these ranges and needn't reach their ends.
Inputs may be any that keep to these rules, and one draw needn't show every extreme that they name: piece_count[o, w] is the number of sea points that ocean device o sends to wave tile w (both numbered latitude band major); in every draw some wave tile receives exactly 4 from every ocean device; the sea cells of tile w number the sum of column w. `piece_offset`: the pieces of one ocean device lie in order of w, do not intersect, and end within its 1024 rows. `sea_mask`: tile w has as many sea cells as the column sum of piece_count for w.
All inputs are finite; a program needn't handle non-finite values.
Results may differ from the reference program's by a relative error of at most 0.0003.
Values sent between devices are 32-bit elements; how exact they have to be, the bound alone decides.
No kernel may reach another device: no remote copies, remote signals or barrier semaphores. Data moves between devices by JAX's collectives and lax.ppermute only.
A program may use at most 192 MiB of HBM per device.

```python
import math
import jax
import jax.numpy as jnp
from jax import lax

NF = 36
ND = 36
CY = 4
CX = 128
SUBSTEPS = 2
CAP = 4
O_DEV = 1024
O_TOTAL = 131072
NY = 32
NX = 2048
N_TY = 8
N_TX = 16
DEVICES = 128


def layout(key):
    folded = jax.random.fold_in(key, 11)
    key_ceiling, key_chosen, key_counts, key_spacing = jax.random.split(folded, 4)
    tile_index = jnp.arange(DEVICES, dtype=jnp.int32)
    chosen = jax.random.randint(key_chosen, (), 0, DEVICES)
    ceiling = jax.random.randint(key_ceiling, (DEVICES,), CAP - CAP // 2, CAP + 1)
    ceiling = jnp.where(tile_index == chosen, CAP, ceiling)
    raw_draw = jax.random.randint(key_counts, (DEVICES, DEVICES), 0, 1 << 20)
    counts = jnp.maximum(ceiling[None, :] - raw_draw % 3, 0)
    counts = jnp.where(tile_index[None, :] == chosen, CAP, counts)
    spacing = jax.random.randint(key_spacing, (DEVICES, DEVICES), 0, CAP + 1)
    extent = counts + spacing
    offsets = jnp.cumsum(extent, axis=1) - extent
    offsets = jnp.where(tile_index[None, :] == DEVICES - 1, O_DEV - CAP, offsets)
    return (counts.astype(jnp.int32), offsets.astype(jnp.int32))


def draw_piece_count(key, part):
    return layout(key)[0]


def draw_piece_offset(key, part):
    return layout(key)[1]


def draw_sea_mask(key, part):
    counts = layout(key)[0]
    sea_cells = jnp.sum(counts, axis=0)
    cell_keys = jax.random.split(jax.random.fold_in(key, 29), DEVICES)
    ranking = jax.vmap(lambda subkey: jax.random.permutation(subkey, CY * CX))(cell_keys)
    marks = (ranking < sea_cells[:, None]).astype(jnp.int32)
    return marks.reshape(N_TY, N_TX, CY, CX).transpose(0, 2, 1, 3).reshape(NY, NX)


def block_levels(rng, shape, shards, low, high):
    def one(axis_at, parts):
        steps = jax.random.uniform(jax.random.fold_in(jax.random.fold_in(rng, 6), axis_at), (parts,), jnp.float32, low / len(shards), high / len(shards))
        return jnp.repeat(jnp.exp(steps), shape[axis_at] // parts).reshape((-1,) + (1,) * (len(shape) - axis_at - 1))

    factor_of = one(*shards[0])
    for cut in shards[1:]:
        factor_of = factor_of * one(*cut)
    return factor_of


def scatter_about(stream_key, shape, width, limit, shards=(), kind=jnp.bfloat16):
    drawn = jax.random.normal(stream_key, shape, jnp.float32) * width
    if len(shards) > 0:
        drawn = block_levels(stream_key, shape, shards, -0.22, 0.18) * drawn
    return jnp.clip(drawn, min=-limit, max=limit).astype(kind)


def setup_inputs(seed: int = 0) -> dict:
    keys = jax.random.split(jax.random.key(seed), 8)
    spectra = jnp.clip(jnp.exp(math.log(2.0) - 3.6888794 * jax.random.uniform(keys[0], (NF, ND, NY, NX), jnp.float32) ** block_levels(keys[0], (NF, ND, NY, NX), ((2, 8), (3, 16)), -0.2, 0.2)), 0.05, 2.0)
    sea_mask = draw_sea_mask(jax.random.fold_in(keys[7], 71), 0)
    currents = scatter_about(keys[2], (2, O_TOTAL), 0.6, 3.6, ((1, 128),), jnp.float32)
    sea_depth = jnp.clip(jnp.exp(math.log(4000.0) - 5.9914645 * jax.random.uniform(keys[3], (O_TOTAL,), jnp.float32) ** block_levels(keys[3], (O_TOTAL,), ((0, 128),), -0.2, 0.2)), 10.0, 4000.0)
    slopes = scatter_about(keys[4], (2, O_TOTAL), 0.003, 0.018, ((1, 128),), jnp.float32)
    piece_offset = draw_piece_offset(jax.random.fold_in(keys[7], 71), 0)
    piece_count = draw_piece_count(jax.random.fold_in(keys[7], 71), 0)
    return {"spectra": spectra, "sea_mask": sea_mask, "currents": currents, "sea_depth": sea_depth, "slopes": slopes, "piece_offset": piece_offset, "piece_count": piece_count}


gravity = 9.81
first_frequency = 0.0418
frequency_ratio = 1.1
time_step = 600.0
cell_metres = 13900.0
refraction_limit = 0.8
land_depth = 1000.0
product_limit = 20.0
group_width = 4

def frequencies(number):
    ordinal = jnp.arange(number, dtype=jnp.float32)
    return first_frequency * jnp.exp(ordinal * math.log(frequency_ratio))

def angles(number):
    heading = jnp.arange(number, dtype=jnp.float32) * (2.0 * math.pi / number)
    return (jnp.cos(heading)[:, None, None], jnp.sin(heading)[:, None, None])

def kinematics(fields, frequency):
    water_depth = jnp.where(fields[5] > 0.5, fields[2], land_depth)
    radian_freq = (2.0 * math.pi * frequency)[:, None, None]
    squared = radian_freq * radian_freq
    initial = squared / (gravity * jnp.sqrt(jnp.tanh(squared * water_depth / gravity)))
    hyperbolic = jnp.tanh(initial * water_depth)
    residue = gravity * initial * hyperbolic - squared
    derivative = gravity * hyperbolic + gravity * initial * water_depth * (1.0 - hyperbolic * hyperbolic)
    wavenumber = initial - residue / derivative
    product = jnp.minimum(wavenumber * water_depth, product_limit)
    double = jnp.sinh(2.0 * product)
    return (radian_freq / wavenumber * (0.5 + product / double), radian_freq / double)

def window(values, offset, length, along):
    return lax.slice_in_dim(values, offset, offset + length, axis=along)

def face_flux(action, courant, sea_layer, along):
    interior = action.shape[along] - 4
    faces = interior + 1
    action_back, action_here, action_next, action_ahead = [window(action, offset, faces, along) for offset in range(4)]
    speed_back, speed_here, speed_next, speed_ahead = [window(courant, offset, faces, along) for offset in range(4)]
    sea_here = window(sea_layer, 1, faces, along - 2)
    sea_next = window(sea_layer, 2, faces, along - 2)
    face_speed = (9.0 * (speed_here + speed_next) - speed_back - speed_ahead) / 16.0 * sea_here * sea_next
    upwind_left = 1.5 * action_here - 0.5 * action_back
    upwind_right = 1.5 * action_next - 0.5 * action_ahead
    through = jnp.maximum(face_speed, 0.0) * upwind_left + jnp.minimum(face_speed, 0.0) * upwind_right
    return window(through, 1, interior, along) - window(through, 0, interior, along)

def advance(row_action, column_action, row_fields, column_fields, frequency):
    dir_count = row_action.shape[1]
    cosine_dir, sine_dir = angles(dir_count)
    row_group, row_turning = kinematics(row_fields, frequency)
    column_group, column_turning = kinematics(column_fields, frequency)
    courant_scale = time_step / cell_metres
    speed_x = (column_group[:, None] * cosine_dir + column_fields[0]) * column_fields[5] * courant_scale
    speed_y = (row_group[:, None] * sine_dir + row_fields[1]) * row_fields[5] * courant_scale
    centre = row_action[:, :, 2:-2]
    shifted = centre - face_flux(column_action, speed_x, column_fields[5], 3) - face_flux(row_action, speed_y, row_fields[5], 2)
    inner_fields = row_fields[:, 2:-2]
    turning = row_turning[:, 2:-2]
    rotation = jnp.clip(turning[:, None] * (sine_dir * inner_fields[3] - cosine_dir * inner_fields[4]) * (time_step * dir_count / (2.0 * math.pi)), -refraction_limit, refraction_limit) * inner_fields[5]
    across = 0.5 * (rotation + jnp.roll(rotation, -1, 1))
    angular_flux = jnp.maximum(across, 0.0) * shifted + jnp.minimum(across, 0.0) * jnp.roll(shifted, -1, 1)
    return (shifted - angular_flux + jnp.roll(angular_flux, 1, 1)) * inner_fields[5]

def propagate(action, row_fields, column_fields):
    total_freqs = action.shape[0]
    groups = total_freqs // group_width
    frequency = frequencies(total_freqs).reshape(groups, group_width)
    blocks = action.reshape((groups, group_width) + action.shape[1:])

    def advance_block(members):
        portion, chosen = members
        rows_padded = jnp.pad(portion, ((0, 0), (0, 0), (2, 2), (0, 0)))
        columns_padded = jnp.concatenate([portion[..., -2:], portion, portion[..., :2]], axis=3)
        return advance(rows_padded, columns_padded, row_fields, column_fields, chosen)
    result = lax.map(advance_block, (blocks, frequency))
    return result.reshape(action.shape)

def couple(currents, sea_depth, slopes, piece_offset, piece_count, sea_mask):
    ocean_table = jnp.concatenate([currents, sea_depth[None], slopes], 0)
    tile_masks = sea_mask.reshape(N_TY, CY, N_TX, CX).transpose(0, 2, 1, 3).reshape(DEVICES, CY * CX)

    def one_tile(members):
        target, flat_mask = members
        incoming = lax.dynamic_index_in_dim(piece_count, target, 1, keepdims=False)
        starting = lax.dynamic_index_in_dim(piece_offset, target, 1, keepdims=False)
        sea_rank = (jnp.cumsum(flat_mask) - 1).astype(jnp.int32)
        ending = jnp.cumsum(incoming).astype(jnp.int32)
        passed = ending[None, :] <= sea_rank[:, None]
        source = jnp.minimum(lax.optimization_barrier(jnp.sum(passed.astype(jnp.int32), 1)).astype(jnp.int32), DEVICES - 1)
        before = lax.optimization_barrier(jnp.sum(jnp.where(passed, incoming[None, :], 0), 1)).astype(jnp.int32)
        global_row = source * O_DEV + jnp.take(starting, source) + sea_rank - before
        global_row = jnp.clip(global_row, 0, DEVICES * O_DEV - 1).astype(jnp.int32)
        return jnp.take(ocean_table, global_row, axis=1) * flat_mask.astype(jnp.float32)[None]
    placed = lax.map(one_tile, (jnp.arange(DEVICES, dtype=jnp.int32), tile_masks))
    return placed.reshape(N_TY, N_TX, 5, CY, CX).transpose(2, 0, 3, 1, 4).reshape(5, NY, NX)

def reference(spectra, sea_mask, currents, sea_depth, slopes, piece_offset, piece_count):
    landed = couple(currents, sea_depth, slopes, piece_offset, piece_count, sea_mask)
    mask_layer = sea_mask.astype(jnp.float32)
    fields = jnp.concatenate([landed, mask_layer[None]], 0)
    row_fields = jnp.pad(fields, ((0, 0), (2, 2), (0, 0)))
    column_fields = jnp.concatenate([fields[..., -2:], fields, fields[..., :2]], axis=2)
    action = spectra * mask_layer
    for substep in range(SUBSTEPS):
        action = propagate(action, row_fields, column_fields)
    return action
```

```python
import functools
import math

import jax
import jax.numpy as jnp
import numpy as np
from jax import lax
from jax.experimental import pallas as pl
from jax.experimental.pallas import tpu as pltpu
from jax.sharding import PartitionSpec as P

NF, ND = 36, 36
BINS = NF * ND
ROWS = BINS + 8
GROUPS = NF // 4
STARTS = (0, 8, 16, 24, 28)

gravity = 9.81
first_frequency = 0.0418
frequency_ratio = 1.1
time_step = 600.0
cell_metres = 13900.0
refraction_limit = 0.8
land_depth = 1000.0
product_limit = 20.0
courant_scale = time_step / cell_metres
turn_scale = time_step * ND / (2.0 * math.pi)

f32, bf16, i32 = jnp.float32, jnp.bfloat16, jnp.int32
HEADING = np.arange(48) % ND * (2.0 * math.pi / ND)
COSINE = np.broadcast_to(np.cos(HEADING)[:, None], (48, 128)).astype(np.float32)
SINE = np.broadcast_to(np.sin(HEADING)[:, None], (48, 128)).astype(np.float32)
SIGMA = (2.0 * math.pi * first_frequency * frequency_ratio ** np.arange(64)).astype(np.float32)
SIGMA_ROWS = np.broadcast_to(SIGMA[:NF, None], (NF, 128)).astype(np.float32)
SIGMA_PACKED = np.where(
    np.arange(16)[:, None] < GROUPS, SIGMA[np.minimum(4 * np.arange(16)[:, None] + np.arange(128)[None, :] // 32, 35)], 1.0
).astype(np.float32)


def roll(x, shift, axis=1):
    size = x.shape[axis]
    if isinstance(shift, int):
        shift %= size
        return x if shift == 0 else pltpu.roll(x, shift, axis)
    return pltpu.roll(x, shift, axis)


def lanes(shape=(8, 128)):
    return lax.broadcasted_iota(i32, shape, len(shape) - 1)


def split3(x):
    high = x.astype(bf16)
    rest = x - high.astype(f32)
    middle = rest.astype(bf16)
    low = (rest - middle.astype(f32)).astype(bf16)
    return jnp.concatenate([high, middle, low], 0)


def dot(a, b):
    return jnp.dot(a, b, preferred_element_type=f32)


def parity():
    return lax.rem(lax.axis_index("ty"), 2)


def planes_kernel(spectra, sea, na, nb, edges):
    flip = parity()
    lane = lanes()
    mask = sea[...].astype(f32)
    for ref in (na, nb):
        for part in range(2):
            ref[part, pl.ds(BINS, 8), :] = jnp.concatenate([mask, jnp.zeros((4, 128), f32)], 0)
    edges[GROUPS, pl.ds(0, 8), :] = jnp.concatenate([mask, jnp.zeros((4, 128), f32)], 0)
    for r in range(8, 40, 8):
        edges[GROUPS, pl.ds(r, 8), :] = jnp.zeros((8, 128), f32)
    row_mask = [jnp.broadcast_to(jnp.where(flip == 1, mask[3 - j : 4 - j], mask[j : j + 1]), (8, 128)) for j in range(4)]
    source = [jnp.where(flip == 1, 3 - j, j) for j in range(4)]

    def group(g, carry):
        for b, start in enumerate(STARTS):
            packed = jnp.zeros((8, 128), f32)
            for q in range(4):
                base = (4 * g + q) * ND + start
                for j in range(4):
                    value = spectra[pl.ds(4 * base + source[j], 8, stride=4), :] * row_mask[j]
                    (na if j < 2 else nb)[j % 2, pl.ds(base, 8), :] = value
                    at = 32 * q + 8 * j
                    packed = jnp.where((lane >= at) & (lane < at + 8), roll(value, at + 4), packed)
            edges[g, pl.ds(8 * b, 8), :] = packed
        return carry

    lax.fori_loop(0, GROUPS, group, 0)


def pieces_kernel(currents, depth, slopes, offset, count, out, rows):
    me = lax.axis_index("ty") * 16 + lax.axis_index("tx")
    table = jnp.concatenate([currents[...], depth[...], slopes[...], jnp.zeros((3, 1024), f32)], 0)
    shifted = jnp.concatenate([roll(table, -s) for s in range(4)], 0)
    wanted = offset[pl.ds(me, 1), :]
    number = count[pl.ds(me, 1), :]
    chosen = (lax.broadcasted_iota(i32, (1024, 128), 0) == wanted).astype(f32).astype(bf16)
    picked = dot(split3(shifted), chosen)
    picked = picked[:32] + picked[32:64] + picked[64:]
    lane = lanes()
    for s in range(4):
        own = jnp.where(number > s, picked[8 * s : 8 * s + 8], 0.0)
        up, down = roll(own, -16), roll(own, 16)
        left = jnp.where(lane % 16 == 0, roll(own, -15), roll(own, 1))
        right = jnp.where(lane % 16 == 15, roll(own, 15), roll(own, -1))
        rows[pl.ds(16 * s, 16), :] = jnp.concatenate(
            [own[:5], up[1:3], down[1:3], left[0:1], left[2:3], right[0:1], right[2:3], jnp.zeros((3, 128), f32)], 0
        )
    rows[pl.ds(64, 64), :] = jnp.zeros((64, 128), f32)
    out[...] = jnp.transpose(rows[...])


def kinematics(water_depth, sigma):
    squared = sigma * sigma
    initial = squared / (gravity * jnp.sqrt(jnp.tanh(squared * water_depth / gravity)))
    hyperbolic = jnp.tanh(initial * water_depth)
    residue = gravity * initial * hyperbolic - squared
    derivative = gravity * hyperbolic + gravity * initial * water_depth * (1.0 - hyperbolic * hyperbolic)
    wavenumber = initial - residue / derivative
    product = jnp.minimum(wavenumber * water_depth, product_limit)
    growth = jnp.exp(2.0 * product)
    double = 0.5 * (growth - 1.0 / growth)
    return sigma / wavenumber * (0.5 + product / double), sigma / double


def pack_edges(rows):
    lane = lanes()
    total = jnp.zeros((8, 128), f32)
    for j, row in enumerate(rows):
        moved = roll(jnp.broadcast_to(row, (8, 128)), 8 * j + 4)
        total = jnp.where((lane >= 8 * j) & (lane < 8 * j + 8), moved, total)
    total = total + roll(total, 32)
    return total + roll(total, 64)


def faces(x, mask, axis):
    ahead = roll(x, -1, axis)
    value = (9.0 * (x + ahead) - roll(x, 1, axis) - roll(x, -2, axis)) * (1.5 / 16.0)
    return value * (mask * roll(mask, -1, axis))


def fields_kernel(
    arrived, count, sea, chip_in, z_in, left_in, right_in, sigma_rows, sigma_packed,
    cgx, cgy, tx, ty, ux, vy, water, edge_cg, edge_u,
):
    flip = parity()
    row, column = lax.axis_index("ty"), lax.axis_index("tx")
    up, down = row * 16 + column + 16, row * 16 + column - 16
    chip = jnp.where(flip == 1, down, up)
    beyond = jnp.where(flip == 1, up, down)
    left = row * 16 + lax.rem(column + 15, 16)
    right = row * 16 + lax.rem(column + 1, 16)
    tile = (row * 16 + column, chip, beyond, left, right)
    lane128 = lanes((128, 128))
    sub128 = lax.broadcasted_iota(i32, (128, 128), 0)
    select = jnp.zeros((128, 128), f32)
    for t in range(5):
        select = jnp.where((lane128 == t) & (sub128 == tile[t]), 1.0, select)
    columns = dot(count[...].astype(f32).astype(bf16), select.astype(bf16))
    below = (lane128 < sub128).astype(f32).astype(bf16)
    first = dot(below, columns.astype(bf16))

    masks = [
        sea[...].astype(f32),
        chip_in[0, pl.ds(BINS, 4), :],
        z_in[0, pl.ds(BINS, 4), :],
        left_in[GROUPS, pl.ds(0, 4), :],
        right_in[GROUPS, pl.ds(0, 4), :],
    ]
    stacked = jnp.concatenate(masks + [jnp.zeros((4, 128), f32)], 0)
    upto = (sub128 <= lane128).astype(f32).astype(bf16)
    prefix = dot(stacked.astype(bf16), upto)
    ranks = []
    for t in range(5):
        before = jnp.zeros((1, 1), f32)
        for r in range(4):
            line = prefix[4 * t + r : 4 * t + r + 1]
            ranks.append(jnp.where(masks[t][r : r + 1] > 0.5, line - 1.0 + before, -2.0))
            before = before + line[:, 127:128]

    def flipped(t, j, table):
        return jnp.where(flip == 1, table[4 * t + 3 - j], table[4 * t + j])

    mask_rows = [masks[t][r : r + 1] for t in range(5) for r in range(4)]
    own_rank = [flipped(0, j, ranks) for j in range(4)]
    own_mask = [flipped(0, j, mask_rows) for j in range(4)]
    chip_rank = [flipped(1, j, ranks) for j in range(2)]
    chip_mask = [flipped(1, j, mask_rows) for j in range(2)]
    z_rank = [flipped(2, 3 - j, ranks) for j in range(2)]
    z_mask = [flipped(2, 3 - j, mask_rows) for j in range(2)]
    left_rank = pack_edges([flipped(3, j, ranks) for j in range(4)])[0:1]
    right_rank = pack_edges([flipped(4, j, ranks) for j in range(4)])[0:1]
    left_mask = pack_edges([flipped(3, j, mask_rows) for j in range(4)])
    right_mask = pack_edges([flipped(4, j, mask_rows) for j in range(4)])

    turned = jnp.transpose(arrived[...])
    values = split3(jnp.concatenate([turned[16 * s : 16 * s + 16] for s in range(4)], 1))

    keys = []
    for t in range(5):
        number, start = columns[:, t : t + 1], first[:, t : t + 1]
        keys.append(
            jnp.concatenate([jnp.where(number > s, start + s, -1.0) for s in range(4)], 0)
        )

    def place(t, rank):
        chosen = (keys[t] == rank).astype(f32).astype(bf16)
        found = dot(values, chosen)
        return found[:16] + found[16:32] + found[32:]

    own = [place(0, own_rank[j]) for j in range(4)]
    near_chip = [place(1, chip_rank[j]) for j in range(2)]
    near_z = [place(2, z_rank[j]) for j in range(2)]
    found_left, found_right = place(3, left_rank), place(4, right_rank)

    def pick(found, chip_side, k):
        use_up = (flip == 0) if chip_side else (flip == 1)
        return jnp.where(use_up, found[5 + k : 6 + k], found[7 + k : 8 + k])

    def stack(rows):
        return jnp.concatenate(rows, 0)

    v8 = stack([pick(near_z[1], False, 0), pick(near_z[0], False, 0)] + [o[1:2] for o in own] + [pick(near_chip[0], True, 0), pick(near_chip[1], True, 0)])
    h8 = stack([pick(near_z[1], False, 1), pick(near_z[0], False, 1)] + [o[2:3] for o in own] + [pick(near_chip[0], True, 1), pick(near_chip[1], True, 1)])
    m8 = stack([z_mask[1], z_mask[0]] + own_mask + [chip_mask[0], chip_mask[1]])
    zero4 = jnp.zeros((4, 128), f32)
    own_m = stack(own_mask + [zero4])
    own_u = stack([o[0:1] for o in own] + [zero4])
    own_sx = stack([o[3:4] for o in own] + [zero4])
    own_sy = stack([o[4:5] for o in own] + [zero4])
    sign = jnp.where(flip == 1, -1.0, 1.0).astype(f32)
    water[...] = own_m
    depth8 = jnp.where(m8 > 0.5, h8, land_depth)
    m8s = m8 * courant_scale
    own_ms = own_m * courant_scale
    ux[...] = faces(own_u * own_ms, own_m, 1)
    vy[...] = roll(faces(v8 * m8s, m8, 0), -1, 0) * sign
    turn_x = own_sx * own_m * (0.5 * turn_scale)
    turn_y = own_sy * own_m * (0.5 * turn_scale)

    def one(f, carry):
        speed, turning = kinematics(depth8, jnp.broadcast_to(sigma_rows[pl.ds(f, 1), :], (8, 128)))
        cgy[f] = roll(faces(speed * m8s, m8, 0), -1, 0) * sign
        cgx[f] = faces(roll(speed, -2, 0) * own_ms, own_m, 1)
        turning = roll(turning, -2, 0)
        tx[f] = turning * turn_x
        ty[f] = turning * turn_y
        return carry

    lax.fori_loop(0, NF, one, 0, unroll=4)

    low = lanes() % 8 < 4
    own_mask_edge = pack_edges(own_mask)
    own_u_edge = pack_edges([o[0:1] for o in own])
    own_h_edge = pack_edges([o[2:3] for o in own])
    for side in range(2):
        outside = low if side == 0 else jnp.logical_not(low)
        found = found_left[9:11] if side == 0 else found_right[11:13]
        mask = jnp.where(outside, left_mask if side == 0 else right_mask, own_mask_edge)
        u = jnp.where(outside, found[0:1], own_u_edge)
        h = jnp.where(outside, found[1:2], own_h_edge)
        depth = jnp.where(mask > 0.5, h, land_depth)
        edge_u[side] = faces(u * (mask * courant_scale), mask, 1)
        for part in range(2):
            speed, _ = kinematics(depth, sigma_packed[pl.ds(8 * part, 8), :])
            edge_cg[side, pl.ds(8 * part, 8), :] = faces(speed * (mask * courant_scale), mask, 1)


def flux(speed, behind, ahead):
    return speed * jnp.where(speed > 0.0, behind, ahead)


def along_x(value, speed):
    third = value * (1.0 / 3.0)
    behind = value - roll(third, 1)
    ahead = roll(value - roll(third, -1), -1)
    through = flux(speed, behind, ahead)
    return through - roll(through, 1)


def step_kernel(
    last, na, nb, z_in, chip_in, edges, left_in, right_in,
    cgx, cgy, tx, ty, ux, vy, water, edge_cg, edge_u, cosine, sine, *rest,
):
    if last:
        out, fix, moved, turn, swirl = rest
    else:
        out_a, out_b, out_edges, fix, moved, turn, swirl = rest
    flip = parity()
    lane = lanes()
    source = [jnp.where(flip == 1, 3 - j, j) for j in range(4)]
    low = lane % 8 < 4

    def edge_group(g, carry):
        for b, start in enumerate(STARTS):
            mine = edges[g, pl.ds(8 * b, 8), :]
            west = jnp.where(low, left_in[g, pl.ds(8 * b, 8), :], mine)
            east = jnp.where(low, mine, right_in[g, pl.ds(8 * b, 8), :])
            c = cosine[pl.ds(start, 8), :]
            change = [
                along_x(value, c * edge_cg[side, pl.ds(g, 1), :] + edge_u[side])
                for side, value in enumerate((west, east))
            ]
            fix[g, pl.ds(8 * b, 8), :] = jnp.where(low, change[1], change[0])
        return carry

    lax.fori_loop(0, GROUPS, edge_group, 0)
    at_edge = (lane < 2) | (lane >= 126)

    def one(g, q):
        f = 4 * g + q
        for b, start in enumerate(STARTS):
            base = f * ND + start
            c, s = cosine[pl.ds(start, 8), :], sine[pl.ds(start, 8), :]
            here = pl.ds(base, 8)
            value = [
                z_in[1, here, :], z_in[0, here, :], na[0, here, :], na[1, here, :],
                nb[0, here, :], nb[1, here, :], chip_in[1, here, :], chip_in[0, here, :],
            ]
            third = [v * (1.0 / 3.0) for v in value]
            across = []
            for k in range(5):
                speed = s * cgy[f, pl.ds(k, 1), :] + vy[pl.ds(k, 1), :]
                across.append(flux(speed, value[k + 1] - third[k], value[k + 2] - third[k + 3]))
            edge = fix[g, pl.ds(8 * b, 8), :]
            for j in range(4):
                speed = c * cgx[f, pl.ds(j, 1), :] + ux[pl.ds(j, 1), :]
                change = along_x(value[j + 2], speed)
                change = jnp.where(at_edge, roll(edge, -(32 * q + 8 * j + 4)), change)
                moved[q, j, pl.ds(8 + start, 8), :] = value[j + 2] - change - (across[j + 1] - across[j])
                half = s * tx[f, pl.ds(j, 1), :] - c * ty[f, pl.ds(j, 1), :]
                turn[q, j, pl.ds(8 + start, 8), :] = jnp.clip(half, -0.5 * refraction_limit, 0.5 * refraction_limit)
        for j in range(4):
            moved[q, j, pl.ds(8 + ND, 1), :] = moved[q, j, pl.ds(8, 1), :]
            turn[q, j, pl.ds(8 + ND, 1), :] = turn[q, j, pl.ds(8, 1), :]
            for start in STARTS:
                speed = turn[q, j, pl.ds(8 + start, 8), :] + turn[q, j, pl.ds(9 + start, 8), :]
                swirl[q, j, pl.ds(8 + start, 8), :] = flux(
                    speed, moved[q, j, pl.ds(8 + start, 8), :], moved[q, j, pl.ds(9 + start, 8), :]
                )
            swirl[q, j, pl.ds(7, 1), :] = swirl[q, j, pl.ds(7 + ND, 1), :]

    def finish(g, q, b):
        f = 4 * g + q
        start = STARTS[b]
        base = f * ND + start
        values = []
        for j in range(4):
            value = (
                moved[q, j, pl.ds(8 + start, 8), :]
                - swirl[q, j, pl.ds(8 + start, 8), :]
                + swirl[q, j, pl.ds(7 + start, 8), :]
            ) * water[pl.ds(j, 1), :]
            if last:
                out[pl.ds(4 * base + source[j], 8, stride=4), :] = value
            else:
                (out_a if j < 2 else out_b)[j % 2, pl.ds(base, 8), :] = value
            values.append(value)
        return values

    def group(g, carry):
        for q in range(4):
            one(g, q)
        for b in range(5):
            packed = jnp.zeros((8, 128), f32)
            for q in range(4):
                for j, value in enumerate(finish(g, q, b)):
                    if not last:
                        at = 32 * q + 8 * j
                        packed = jnp.where((lane >= at) & (lane < at + 8), roll(value, at + 4), packed)
            if not last:
                out_edges[g, pl.ds(8 * b, 8), :] = packed
        return carry

    lax.fori_loop(0, GROUPS, group, 0)


def shape(*dims, dtype=f32):
    return jax.ShapeDtypeStruct(dims, dtype)


def call(kernel, out, name, scratch=(), cost=2_000_000, moved=4_000_000):
    return pl.pallas_call(
        kernel,
        out_shape=out,
        scratch_shapes=list(scratch),
        name=name,
        cost_estimate=pl.CostEstimate(flops=cost, bytes_accessed=moved, transcendentals=0),
    )


PLANE = shape(2, ROWS, 128)
EDGES = shape(GROUPS + 1, 40, 128)
STEP_SCRATCH = [pltpu.VMEM((GROUPS, 40, 128), f32)] + [pltpu.VMEM((4, 4, 56, 128), f32)] * 3


def exchange(na, nb, edges):
    z_pairs = [p for z in range(3) for p in ((2 * z + 1, 2 * z + 2), (2 * z + 2, 2 * z + 1))]
    chip_pairs = [p for z in range(4) for p in ((2 * z, 2 * z + 1), (2 * z + 1, 2 * z))]
    east = [(i, (i + 1) % 16) for i in range(16)]
    west = [((i + 1) % 16, i) for i in range(16)]
    z_in = lax.ppermute(na, "ty", z_pairs)
    chip_in = lax.ppermute(nb, "ty", chip_pairs)
    left_in = lax.ppermute(edges, "tx", east)
    right_in = lax.ppermute(edges, "tx", west)
    return z_in, chip_in, left_in, right_in


def on_device(spectra, sea_mask, currents, sea_depth, slopes, piece_offset, piece_count):
    flat = spectra.reshape(4 * BINS, 128)
    pieces = call(pieces_kernel, shape(128, 128), "pieces", [pltpu.VMEM((128, 128), f32)])(
        currents, sea_depth.reshape(1, 1024), slopes, piece_offset, piece_count
    )
    na, nb, edges = call(planes_kernel, (PLANE, PLANE, EDGES), "planes")(flat, sea_mask)
    z_in, chip_in, left_in, right_in = exchange(na, nb, edges)
    arrived = lax.all_to_all(pieces, ("ty", "tx"), split_axis=0, concat_axis=0, tiled=True)
    per_frequency = shape(NF, 8, 128)
    speeds = call(
        fields_kernel,
        (per_frequency,) * 4 + (shape(8, 128),) * 3 + (shape(2, 16, 128), shape(2, 8, 128)),
        "fields",
    )(arrived, piece_count, sea_mask, chip_in, z_in, left_in, right_in, SIGMA_ROWS, SIGMA_PACKED)
    na, nb, own_edges = call(
        functools.partial(step_kernel, False), (PLANE, PLANE, EDGES), "step_one", STEP_SCRATCH
    )(na, nb, z_in, chip_in, edges, left_in, right_in, *speeds, COSINE, SINE)
    z_in, chip_in, left_in, right_in = exchange(na, nb, own_edges)
    out = call(functools.partial(step_kernel, True), shape(4 * BINS, 128), "step_two", STEP_SCRATCH)(
        na, nb, z_in, chip_in, own_edges, left_in, right_in, *speeds, COSINE, SINE
    )
    return out.reshape(spectra.shape)


def solution(mesh):
    return jax.shard_map(
        on_device,
        mesh=mesh,
        in_specs=(
            P(None, None, "ty", "tx"),
            P("ty", "tx"),
            P(None, ("ty", "tx")),
            P(("ty", "tx")),
            P(None, ("ty", "tx")),
            P(),
            P(),
        ),
        out_specs=P(None, None, "ty", "tx"),
        check_vma=False,
    )
```

```python
import functools
import math

import jax
import jax.numpy as jnp
import numpy as np
from jax import lax
from jax.experimental import pallas as pl
from jax.experimental.pallas import tpu as pltpu
from jax.sharding import PartitionSpec as P

NF, ND = 36, 36
BINS = NF * ND
ROWS = BINS + 8
GROUPS = NF // 4
STARTS = (0, 8, 16, 24, 28)

gravity = 9.81
first_frequency = 0.0418
frequency_ratio = 1.1
time_step = 600.0
cell_metres = 13900.0
refraction_limit = 0.8
land_depth = 1000.0
product_limit = 20.0
courant_scale = time_step / cell_metres
turn_scale = time_step * ND / (2.0 * math.pi)

f32, bf16, i32 = jnp.float32, jnp.bfloat16, jnp.int32
HEADING = np.arange(48) % ND * (2.0 * math.pi / ND)
COSINE = np.broadcast_to(np.cos(HEADING)[:, None], (48, 128)).astype(np.float32)
SINE = np.broadcast_to(np.sin(HEADING)[:, None], (48, 128)).astype(np.float32)
SIGMA = (2.0 * math.pi * first_frequency * frequency_ratio ** np.arange(64)).astype(np.float32)
SIGMA_ROWS = np.broadcast_to(SIGMA[:NF, None], (NF, 128)).astype(np.float32)
SIGMA_PACKED = np.where(
    np.arange(16)[:, None] < GROUPS, SIGMA[np.minimum(4 * np.arange(16)[:, None] + np.arange(128)[None, :] // 32, 35)], 1.0
).astype(np.float32)


def roll(x, shift, axis=1):
    size = x.shape[axis]
    if isinstance(shift, int):
        shift %= size
        return x if shift == 0 else pltpu.roll(x, shift, axis)
    return pltpu.roll(x, shift, axis)


def lanes(shape=(8, 128)):
    return lax.broadcasted_iota(i32, shape, len(shape) - 1)


def split3(x):
    high = x.astype(bf16)
    rest = x - high.astype(f32)
    middle = rest.astype(bf16)
    low = (rest - middle.astype(f32)).astype(bf16)
    return jnp.concatenate([high, middle, low], 0)


def dot(a, b):
    return jnp.dot(a, b, preferred_element_type=f32)


def parity():
    return lax.rem(lax.axis_index("ty"), 2)


def planes_kernel(spectra, sea, na, nb, edges):
    flip = parity()
    mask = sea[...].astype(f32)
    for ref in (na, nb):
        for part in range(2):
            ref[part, pl.ds(BINS, 8), :] = jnp.concatenate([mask, jnp.zeros((4, 128), f32)], 0)
    edges[GROUPS, pl.ds(0, 8), :] = jnp.concatenate([mask, jnp.zeros((4, 128), f32)], 0)
    for r in range(8, 40, 8):
        edges[GROUPS, pl.ds(r, 8), :] = jnp.zeros((8, 128), f32)
    row_mask = [jnp.broadcast_to(jnp.where(flip == 1, mask[3 - j : 4 - j], mask[j : j + 1]), (8, 128)) for j in range(4)]
    source = [jnp.where(flip == 1, 3 - j, j) for j in range(4)]

    def group(g, carry):
        for k in range(18):
            base = 144 * g + 8 * k
            for j in range(4):
                (na if j < 2 else nb)[j % 2, pl.ds(base, 8), :] = (
                    spectra[pl.ds(4 * base + source[j], 8, stride=4), :] * row_mask[j]
                )
        return carry

    lax.fori_loop(0, GROUPS, group, 0)
    pack_planes(na, nb, edges)


def pack_planes(na, nb, edges):
    lane = lanes()

    def group(g, carry):
        for b, start in enumerate(STARTS):
            packed = jnp.zeros((8, 128), f32)
            for q in range(4):
                for j in range(4):
                    value = (na if j < 2 else nb)[j % 2, pl.ds((4 * g + q) * ND + start, 8), :]
                    at = 32 * q + 8 * j
                    packed = jnp.where((lane >= at) & (lane < at + 8), roll(value, at + 4), packed)
            edges[g, pl.ds(8 * b, 8), :] = packed
        return carry

    lax.fori_loop(0, GROUPS, group, 0)


def pieces_kernel(currents, depth, slopes, offset, count, out, rows):
    me = lax.axis_index("ty") * 16 + lax.axis_index("tx")
    table = jnp.concatenate([currents[...], depth[...], slopes[...], jnp.zeros((3, 1024), f32)], 0)
    shifted = jnp.concatenate([roll(table, -s) for s in range(4)], 0)
    wanted = offset[pl.ds(me, 1), :]
    number = count[pl.ds(me, 1), :]
    chosen = (lax.broadcasted_iota(i32, (1024, 128), 0) == wanted).astype(f32).astype(bf16)
    picked = dot(split3(shifted), chosen)
    picked = picked[:32] + picked[32:64] + picked[64:]
    lane = lanes()
    for s in range(4):
        own = jnp.where(number > s, picked[8 * s : 8 * s + 8], 0.0)
        up, down = roll(own, -16), roll(own, 16)
        left = jnp.where(lane % 16 == 0, roll(own, -15), roll(own, 1))
        right = jnp.where(lane % 16 == 15, roll(own, 15), roll(own, -1))
        rows[pl.ds(16 * s, 16), :] = jnp.concatenate(
            [own[:5], up[1:3], down[1:3], left[0:1], left[2:3], right[0:1], right[2:3], jnp.zeros((3, 128), f32)], 0
        )
    rows[pl.ds(64, 64), :] = jnp.zeros((64, 128), f32)
    out[...] = jnp.transpose(rows[...])


def kinematics(water_depth, sigma):
    squared = sigma * sigma
    initial = squared / (gravity * jnp.sqrt(jnp.tanh(squared * water_depth / gravity)))
    hyperbolic = jnp.tanh(initial * water_depth)
    residue = gravity * initial * hyperbolic - squared
    derivative = gravity * hyperbolic + gravity * initial * water_depth * (1.0 - hyperbolic * hyperbolic)
    wavenumber = initial - residue / derivative
    product = jnp.minimum(wavenumber * water_depth, product_limit)
    growth = jnp.exp(2.0 * product)
    double = 0.5 * (growth - 1.0 / growth)
    return sigma / wavenumber * (0.5 + product / double), sigma / double


def pack_edges(rows):
    lane = lanes()
    total = jnp.zeros((8, 128), f32)
    for j, row in enumerate(rows):
        moved = roll(jnp.broadcast_to(row, (8, 128)), 8 * j + 4)
        total = jnp.where((lane >= 8 * j) & (lane < 8 * j + 8), moved, total)
    total = total + roll(total, 32)
    return total + roll(total, 64)


def faces(x, mask, axis):
    ahead = roll(x, -1, axis)
    value = (9.0 * (x + ahead) - roll(x, 1, axis) - roll(x, -2, axis)) * (1.5 / 16.0)
    return value * (mask * roll(mask, -1, axis))


def fields_kernel(
    arrived, count, sea, chip_in, z_in, left_in, right_in, sigma_rows, sigma_packed,
    cgx, cgy, tx, ty, ux, vy, water, edge_cg, edge_u,
):
    flip = parity()
    row, column = lax.axis_index("ty"), lax.axis_index("tx")
    up, down = row * 16 + column + 16, row * 16 + column - 16
    chip = jnp.where(flip == 1, down, up)
    beyond = jnp.where(flip == 1, up, down)
    left = row * 16 + lax.rem(column + 15, 16)
    right = row * 16 + lax.rem(column + 1, 16)
    tile = (row * 16 + column, chip, beyond, left, right)
    lane128 = lanes((128, 128))
    sub128 = lax.broadcasted_iota(i32, (128, 128), 0)
    select = jnp.zeros((128, 128), f32)
    for t in range(5):
        select = jnp.where((lane128 == t) & (sub128 == tile[t]), 1.0, select)
    columns = dot(count[...].astype(f32).astype(bf16), select.astype(bf16))
    below = (lane128 < sub128).astype(f32).astype(bf16)
    first = dot(below, columns.astype(bf16))

    masks = [
        sea[...].astype(f32),
        chip_in[0, pl.ds(BINS, 4), :],
        z_in[0, pl.ds(BINS, 4), :],
        left_in[GROUPS, pl.ds(0, 4), :],
        right_in[GROUPS, pl.ds(0, 4), :],
    ]
    stacked = jnp.concatenate(masks + [jnp.zeros((4, 128), f32)], 0)
    upto = (sub128 <= lane128).astype(f32).astype(bf16)
    prefix = dot(stacked.astype(bf16), upto)
    ranks = []
    for t in range(5):
        before = jnp.zeros((1, 1), f32)
        for r in range(4):
            line = prefix[4 * t + r : 4 * t + r + 1]
            ranks.append(jnp.where(masks[t][r : r + 1] > 0.5, line - 1.0 + before, -2.0))
            before = before + line[:, 127:128]

    def flipped(t, j, table):
        return jnp.where(flip == 1, table[4 * t + 3 - j], table[4 * t + j])

    mask_rows = [masks[t][r : r + 1] for t in range(5) for r in range(4)]
    own_rank = [flipped(0, j, ranks) for j in range(4)]
    own_mask = [flipped(0, j, mask_rows) for j in range(4)]
    chip_rank = [flipped(1, j, ranks) for j in range(2)]
    chip_mask = [flipped(1, j, mask_rows) for j in range(2)]
    z_rank = [flipped(2, 3 - j, ranks) for j in range(2)]
    z_mask = [flipped(2, 3 - j, mask_rows) for j in range(2)]
    left_rank = pack_edges([flipped(3, j, ranks) for j in range(4)])[0:1]
    right_rank = pack_edges([flipped(4, j, ranks) for j in range(4)])[0:1]
    left_mask = pack_edges([flipped(3, j, mask_rows) for j in range(4)])
    right_mask = pack_edges([flipped(4, j, mask_rows) for j in range(4)])

    turned = jnp.transpose(arrived[...])
    values = split3(jnp.concatenate([turned[16 * s : 16 * s + 16] for s in range(4)], 1))

    keys = []
    for t in range(5):
        number, start = columns[:, t : t + 1], first[:, t : t + 1]
        keys.append(
            jnp.concatenate([jnp.where(number > s, start + s, -1.0) for s in range(4)], 0)
        )

    def place(t, rank):
        chosen = (keys[t] == rank).astype(f32).astype(bf16)
        found = dot(values, chosen)
        return found[:16] + found[16:32] + found[32:]

    own = [place(0, own_rank[j]) for j in range(4)]
    near_chip = [place(1, chip_rank[j]) for j in range(2)]
    near_z = [place(2, z_rank[j]) for j in range(2)]
    found_left, found_right = place(3, left_rank), place(4, right_rank)

    def pick(found, chip_side, k):
        use_up = (flip == 0) if chip_side else (flip == 1)
        return jnp.where(use_up, found[5 + k : 6 + k], found[7 + k : 8 + k])

    def stack(rows):
        return jnp.concatenate(rows, 0)

    v8 = stack([pick(near_z[1], False, 0), pick(near_z[0], False, 0)] + [o[1:2] for o in own] + [pick(near_chip[0], True, 0), pick(near_chip[1], True, 0)])
    h8 = stack([pick(near_z[1], False, 1), pick(near_z[0], False, 1)] + [o[2:3] for o in own] + [pick(near_chip[0], True, 1), pick(near_chip[1], True, 1)])
    m8 = stack([z_mask[1], z_mask[0]] + own_mask + [chip_mask[0], chip_mask[1]])
    zero4 = jnp.zeros((4, 128), f32)
    own_m = stack(own_mask + [zero4])
    own_u = stack([o[0:1] for o in own] + [zero4])
    own_sx = stack([o[3:4] for o in own] + [zero4])
    own_sy = stack([o[4:5] for o in own] + [zero4])
    sign = jnp.where(flip == 1, -1.0, 1.0).astype(f32)
    water[...] = own_m
    depth8 = jnp.where(m8 > 0.5, h8, land_depth)
    m8s = m8 * courant_scale
    own_ms = own_m * courant_scale
    ux[...] = faces(own_u * own_ms, own_m, 1)
    vy[...] = roll(faces(v8 * m8s, m8, 0), -1, 0) * sign
    turn_x = own_sx * own_m * (0.5 * turn_scale)
    turn_y = own_sy * own_m * (0.5 * turn_scale)

    def one(f, carry):
        speed, turning = kinematics(depth8, jnp.broadcast_to(sigma_rows[pl.ds(f, 1), :], (8, 128)))
        cgy[f] = roll(faces(speed * m8s, m8, 0), -1, 0) * sign
        cgx[f] = faces(roll(speed, -2, 0) * own_ms, own_m, 1)
        turning = roll(turning, -2, 0)
        tx[f] = turning * turn_x
        ty[f] = turning * turn_y
        return carry

    lax.fori_loop(0, NF, one, 0, unroll=4)

    low = lanes() % 8 < 4
    own_mask_edge = pack_edges(own_mask)
    own_u_edge = pack_edges([o[0:1] for o in own])
    own_h_edge = pack_edges([o[2:3] for o in own])
    for side in range(2):
        outside = low if side == 0 else jnp.logical_not(low)
        found = found_left[9:11] if side == 0 else found_right[11:13]
        mask = jnp.where(outside, left_mask if side == 0 else right_mask, own_mask_edge)
        u = jnp.where(outside, found[0:1], own_u_edge)
        h = jnp.where(outside, found[1:2], own_h_edge)
        depth = jnp.where(mask > 0.5, h, land_depth)
        edge_u[side] = faces(u * (mask * courant_scale), mask, 1)
        for part in range(2):
            speed, _ = kinematics(depth, sigma_packed[pl.ds(8 * part, 8), :])
            edge_cg[side, pl.ds(8 * part, 8), :] = faces(speed * (mask * courant_scale), mask, 1)


def flux(speed, behind, ahead):
    return speed * jnp.where(speed > 0.0, behind, ahead)


def through_east(value, speed):
    third = 1.0 / 3.0
    return flux(speed, value - roll(value, 1) * third, roll(value, -1) - roll(value, -2) * third)


def step_kernel(
    last, na, nb, z_in, chip_in, edges, left_in, right_in,
    cgx, cgy, tx, ty, ux, vy, water, edge_cg, edge_u, cosine, sine, *rest,
):
    if last:
        out, edge_flux, fix, east, moved, turn, swirl = rest
    else:
        out_a, out_b, out_edges, edge_flux, fix, east, moved, turn, swirl = rest
    flip = parity()
    lane = lanes()
    source = [jnp.where(flip == 1, 3 - j, j) for j in range(4)]
    low = lane % 8 < 4

    def edge_group(g, carry):
        for b, start in enumerate(STARTS):
            mine = edges[g, pl.ds(8 * b, 8), :]
            left = jnp.where(low, left_in[g, pl.ds(8 * b, 8), :], mine)
            right = jnp.where(low, mine, right_in[g, pl.ds(8 * b, 8), :])
            c = cosine[pl.ds(start, 8), :]
            for side, value in enumerate((left, right)):
                speed = c * edge_cg[side, pl.ds(g, 1), :] + edge_u[side]
                edge_flux[side, g, pl.ds(8 * b, 8), :] = through_east(value, speed)
        return carry

    lax.fori_loop(0, GROUPS, edge_group, 0)

    def x_group(g, carry):
        for q in range(4):
            f = 4 * g + q
            for start in STARTS:
                here = pl.ds(f * ND + start, 8)
                c = cosine[pl.ds(start, 8), :]
                for j in range(4):
                    value = (na if j < 2 else nb)[j % 2, here, :]
                    east[j, here, :] = through_east(value, c * cgx[f, pl.ds(j, 1), :] + ux[pl.ds(j, 1), :])
        return carry

    lax.fori_loop(0, GROUPS, x_group, 0)

    def fix_group(g, carry):
        for b in range(5):
            here = pl.ds(8 * b, 8)
            left, right = edge_flux[0, g, here, :], edge_flux[1, g, here, :]
            fix[g, here, :] = jnp.where(low, right - roll(right, 1), left - roll(left, 1))
        return carry

    lax.fori_loop(0, GROUPS, fix_group, 0)
    at_edge = (lane < 2) | (lane >= 126)

    def one(g, q):
        f = 4 * g + q
        for b, start in enumerate(STARTS):
            base = f * ND + start
            c, s = cosine[pl.ds(start, 8), :], sine[pl.ds(start, 8), :]
            here = pl.ds(base, 8)
            value = [
                z_in[1, here, :], z_in[0, here, :], na[0, here, :], na[1, here, :],
                nb[0, here, :], nb[1, here, :], chip_in[1, here, :], chip_in[0, here, :],
            ]
            third = [v * (1.0 / 3.0) for v in value]
            across = []
            for k in range(5):
                speed = s * cgy[f, pl.ds(k, 1), :] + vy[pl.ds(k, 1), :]
                across.append(flux(speed, value[k + 1] - third[k], value[k + 2] - third[k + 3]))
            edge = fix[g, pl.ds(8 * b, 8), :]
            for j in range(4):
                through = east[j, here, :]
                change = jnp.where(at_edge, roll(edge, -(32 * q + 8 * j + 4)), through - roll(through, 1))
                moved[q, j, pl.ds(8 + start, 8), :] = value[j + 2] - change - (across[j + 1] - across[j])
                half = s * tx[f, pl.ds(j, 1), :] - c * ty[f, pl.ds(j, 1), :]
                turn[q, j, pl.ds(8 + start, 8), :] = jnp.clip(half, -0.5 * refraction_limit, 0.5 * refraction_limit)
        for j in range(4):
            moved[q, j, pl.ds(8 + ND, 1), :] = moved[q, j, pl.ds(8, 1), :]
            turn[q, j, pl.ds(8 + ND, 1), :] = turn[q, j, pl.ds(8, 1), :]
            for start in STARTS:
                speed = turn[q, j, pl.ds(8 + start, 8), :] + turn[q, j, pl.ds(9 + start, 8), :]
                swirl[q, j, pl.ds(8 + start, 8), :] = flux(
                    speed, moved[q, j, pl.ds(8 + start, 8), :], moved[q, j, pl.ds(9 + start, 8), :]
                )
            swirl[q, j, pl.ds(7, 1), :] = swirl[q, j, pl.ds(7 + ND, 1), :]

    def finish(g, q, b):
        start = STARTS[b]
        base = (4 * g + q) * ND + start
        for j in range(4):
            value = (
                moved[q, j, pl.ds(8 + start, 8), :]
                - swirl[q, j, pl.ds(8 + start, 8), :]
                + swirl[q, j, pl.ds(7 + start, 8), :]
            ) * water[pl.ds(j, 1), :]
            if last:
                out[pl.ds(4 * base + source[j], 8, stride=4), :] = value
            else:
                (out_a if j < 2 else out_b)[j % 2, pl.ds(base, 8), :] = value

    def group(g, carry):
        for q in range(4):
            one(g, q)
        for q in range(4):
            for b in range(5):
                finish(g, q, b)
        return carry

    lax.fori_loop(0, GROUPS, group, 0)
    if not last:
        pack_planes(out_a, out_b, out_edges)


def shape(*dims, dtype=f32):
    return jax.ShapeDtypeStruct(dims, dtype)


def call(kernel, out, name, scratch=(), limit=24, cost=2_000_000, moved=4_000_000):
    return pl.pallas_call(
        kernel,
        out_shape=out,
        scratch_shapes=list(scratch),
        name=name,
        compiler_params=pltpu.CompilerParams(vmem_limit_bytes=limit << 20),
        cost_estimate=pl.CostEstimate(flops=cost, bytes_accessed=moved, transcendentals=0),
    )


PLANE = shape(2, ROWS, 128)
EDGES = shape(GROUPS + 1, 40, 128)
STEP_SCRATCH = [pltpu.VMEM((2, GROUPS, 40, 128), f32), pltpu.VMEM((GROUPS, 40, 128), f32), pltpu.VMEM((4, BINS, 128), f32)] + [pltpu.VMEM((4, 4, 56, 128), f32)] * 3


def exchange(na, nb, edges):
    z_pairs = [p for z in range(3) for p in ((2 * z + 1, 2 * z + 2), (2 * z + 2, 2 * z + 1))]
    chip_pairs = [p for z in range(4) for p in ((2 * z, 2 * z + 1), (2 * z + 1, 2 * z))]
    east = [(i, (i + 1) % 16) for i in range(16)]
    west = [((i + 1) % 16, i) for i in range(16)]
    z_in = lax.ppermute(na, "ty", z_pairs)
    chip_in = lax.ppermute(nb, "ty", chip_pairs)
    left_in = lax.ppermute(edges, "tx", east)
    right_in = lax.ppermute(edges, "tx", west)
    return z_in, chip_in, left_in, right_in


def on_device(spectra, sea_mask, currents, sea_depth, slopes, piece_offset, piece_count):
    flat = spectra.reshape(4 * BINS, 128)
    pieces = call(pieces_kernel, shape(128, 128), "pieces", [pltpu.VMEM((128, 128), f32)])(
        currents, sea_depth.reshape(1, 1024), slopes, piece_offset, piece_count
    )
    na, nb, edges = call(planes_kernel, (PLANE, PLANE, EDGES), "planes")(flat, sea_mask)
    z_in, chip_in, left_in, right_in = exchange(na, nb, edges)
    arrived = lax.all_to_all(pieces, ("ty", "tx"), split_axis=0, concat_axis=0, tiled=True)
    per_frequency = shape(NF, 8, 128)
    speeds = call(
        fields_kernel,
        (per_frequency,) * 4 + (shape(8, 128),) * 3 + (shape(2, 16, 128), shape(2, 8, 128)),
        "fields",
    )(arrived, piece_count, sea_mask, chip_in, z_in, left_in, right_in, SIGMA_ROWS, SIGMA_PACKED)
    na, nb, own_edges = call(
        functools.partial(step_kernel, False), (PLANE, PLANE, EDGES), "step_one", STEP_SCRATCH
    )(na, nb, z_in, chip_in, edges, left_in, right_in, *speeds, COSINE, SINE)
    z_in, chip_in, left_in, right_in = exchange(na, nb, own_edges)
    out = call(functools.partial(step_kernel, True), shape(4 * BINS, 128), "step_two", STEP_SCRATCH)(
        na, nb, z_in, chip_in, own_edges, left_in, right_in, *speeds, COSINE, SINE
    )
    return out.reshape(spectra.shape)


def solution(mesh):
    return jax.shard_map(
        on_device,
        mesh=mesh,
        in_specs=(
            P(None, None, "ty", "tx"),
            P("ty", "tx"),
            P(None, ("ty", "tx")),
            P(("ty", "tx")),
            P(None, ("ty", "tx")),
            P(),
            P(),
        ),
        out_specs=P(None, None, "ty", "tx"),
        check_vma=False,
    )
```

```python
import functools
import math

import jax
import jax.numpy as jnp
import numpy as np
from jax import lax
from jax.experimental import pallas as pl
from jax.experimental.pallas import tpu as pltpu
from jax.sharding import PartitionSpec as P


NF, ND = 36, 36
BINS = NF * ND
ROWS = BINS + 8
GROUPS = NF // 4
STARTS = (0, 8, 16, 24, 28)

gravity = 9.81
first_frequency = 0.0418
frequency_ratio = 1.1
time_step = 600.0
cell_metres = 13900.0
refraction_limit = 0.8
land_depth = 1000.0
product_limit = 20.0
courant_scale = time_step / cell_metres
turn_scale = time_step * ND / (2.0 * math.pi)

f32, bf16, i32 = jnp.float32, jnp.bfloat16, jnp.int32
HEADING = np.arange(48) % ND * (2.0 * math.pi / ND)
COSINE = np.broadcast_to(np.cos(HEADING)[:, None], (48, 128)).astype(np.float32)
SINE = np.broadcast_to(np.sin(HEADING)[:, None], (48, 128)).astype(np.float32)
SIGMA = (2.0 * math.pi * first_frequency * frequency_ratio ** np.arange(64)).astype(np.float32)
SIGMA_ROWS = np.broadcast_to(SIGMA[:NF, None], (NF, 128)).astype(np.float32)
SIGMA_PACKED = np.where(
    np.arange(16)[:, None] < GROUPS, SIGMA[np.minimum(4 * np.arange(16)[:, None] + np.arange(128)[None, :] // 32, 35)], 1.0
).astype(np.float32)


def roll(x, shift, axis=1):
    size = x.shape[axis]
    if isinstance(shift, int):
        shift %= size
        return x if shift == 0 else pltpu.roll(x, shift, axis)
    return pltpu.roll(x, shift, axis)


def lanes(shape=(8, 128)):
    return lax.broadcasted_iota(i32, shape, len(shape) - 1)


def split3(x):
    high = x.astype(bf16)
    rest = x - high.astype(f32)
    middle = rest.astype(bf16)
    low = (rest - middle.astype(f32)).astype(bf16)
    return jnp.concatenate([high, middle, low], 0)


def dot(a, b):
    return jnp.dot(a, b, preferred_element_type=f32)


def parity():
    return lax.rem(lax.axis_index("ty"), 2)


def planes_kernel(spectra, sea, na, nb, edges, to_east, to_west):
    flip = parity()
    mask = sea[...].astype(f32)
    tail = jnp.concatenate([mask, jnp.zeros((4, 128), f32)], 0)
    for part in range(2):
        na[part, pl.ds(BINS, 8), :] = tail
        nb[part, pl.ds(BINS, 8), :] = tail
    to_east[0, pl.ds(40, 8), :] = tail
    to_west[0, pl.ds(40, 8), :] = tail
    row_mask = [jnp.broadcast_to(jnp.where(flip == 1, mask[3 - j : 4 - j], mask[j : j + 1]), (8, 128)) for j in range(4)]
    source = [jnp.where(flip == 1, 3 - j, j) for j in range(4)]

    def group(g, carry):
        for k in range(18):
            base = 144 * g + 8 * k
            for j in range(4):
                (na if j < 2 else nb)[j % 2, pl.ds(base, 8), :] = (
                    spectra[pl.ds(4 * base + source[j], 8, stride=4), :] * row_mask[j]
                )
        return carry

    lax.fori_loop(0, GROUPS, group, 0)
    pack_planes(na, nb, edges)
    pack_sends(edges, to_east, to_west)


def pack_planes(na, nb, edges):
    lane = lanes()

    def group(g, carry):
        for b, start in enumerate(STARTS):
            packed = jnp.zeros((8, 128), f32)
            for q in range(4):
                for j in range(4):
                    value = (na if j < 2 else nb)[j % 2, pl.ds((4 * g + q) * ND + start, 8), :]
                    at = 32 * q + 8 * j
                    packed = jnp.where((lane >= at) & (lane < at + 8), roll(value, at + 4), packed)
            edges[g, pl.ds(8 * b, 8), :] = packed
        return carry

    lax.fori_loop(0, GROUPS, group, 0)


SHIFTS = (0, 2, 4, -2)


def place_of(first, g):
    return lanes() % 8 // 2 == (first + SHIFTS[g % 4]) % 8 // 2


def pack_sends(edges, to_east, to_west):
    for b in range(5):
        here = pl.ds(8 * b, 8)
        for first in range(0, GROUPS, 4):
            east, west = jnp.zeros((8, 128), f32), jnp.zeros((8, 128), f32)
            for g in range(first, min(first + 4, GROUPS)):
                value = roll(edges[g, here, :], SHIFTS[g % 4])
                east = jnp.where(place_of(2, g), value, east)
                west = jnp.where(place_of(4, g), value, west)
            to_east[first // 4, here, :] = east
            to_west[first // 4, here, :] = west


def unpack_sends(edges, left_in, right_in, halo):
    c = lanes() % 8 // 2
    for b in range(5):
        here = pl.ds(8 * b, 8)
        for g in range(GROUPS):
            mine = edges[g, here, :]
            halo[0, g, here, :] = jnp.where(c == 1, roll(left_in[g // 4, here, :], -SHIFTS[g % 4]), mine)
            halo[1, g, here, :] = jnp.where(c == 2, roll(right_in[g // 4, here, :], -SHIFTS[g % 4]), mine)


def pieces_kernel(currents, depth, slopes, offset, count, out, rows):
    me = lax.axis_index("ty") * 16 + lax.axis_index("tx")
    table = jnp.concatenate([currents[...], depth[...], slopes[...], jnp.zeros((3, 1024), f32)], 0)
    shifted = jnp.concatenate([roll(table, -s) for s in range(4)], 0)
    wanted = offset[pl.ds(me, 1), :]
    number = count[pl.ds(me, 1), :]
    chosen = (lax.broadcasted_iota(i32, (1024, 128), 0) == wanted).astype(f32).astype(bf16)
    picked = dot(split3(shifted), chosen)
    picked = picked[:32] + picked[32:64] + picked[64:]
    lane = lanes()
    for s in range(4):
        own = jnp.where(number > s, picked[8 * s : 8 * s + 8], 0.0)
        up, down = roll(own, -16), roll(own, 16)
        left = jnp.where(lane % 16 == 0, roll(own, -15), roll(own, 1))
        right = jnp.where(lane % 16 == 15, roll(own, 15), roll(own, -1))
        rows[pl.ds(16 * s, 16), :] = jnp.concatenate(
            [own[:5], up[1:3], down[1:3], left[0:1], left[2:3], right[0:1], right[2:3], jnp.zeros((3, 128), f32)], 0
        )
    rows[pl.ds(64, 64), :] = jnp.zeros((64, 128), f32)
    out[...] = jnp.transpose(rows[...])


def kinematics(water_depth, sigma):
    squared = sigma * sigma
    initial = squared / (gravity * jnp.sqrt(jnp.tanh(squared * water_depth / gravity)))
    hyperbolic = jnp.tanh(initial * water_depth)
    residue = gravity * initial * hyperbolic - squared
    derivative = gravity * hyperbolic + gravity * initial * water_depth * (1.0 - hyperbolic * hyperbolic)
    wavenumber = initial - residue / derivative
    product = jnp.minimum(wavenumber * water_depth, product_limit)
    growth = jnp.exp(2.0 * product)
    double = 0.5 * (growth - 1.0 / growth)
    return sigma / wavenumber * (0.5 + product / double), sigma / double


def pack_edges(rows):
    lane = lanes()
    total = jnp.zeros((8, 128), f32)
    for j, row in enumerate(rows):
        moved = roll(jnp.broadcast_to(row, (8, 128)), 8 * j + 4)
        total = jnp.where((lane >= 8 * j) & (lane < 8 * j + 8), moved, total)
    total = total + roll(total, 32)
    return total + roll(total, 64)


def faces(x, mask, axis):
    ahead = roll(x, -1, axis)
    value = (9.0 * (x + ahead) - roll(x, 1, axis) - roll(x, -2, axis)) * (1.5 / 16.0)
    return value * (mask * roll(mask, -1, axis))


def fields_kernel(
    arrived, count, sea, chip_in, z_in, left_in, right_in, sigma_rows, sigma_packed,
    cgx, cgy, tx, ty, ux, vy, water, edge_cg, edge_u,
):
    flip = parity()
    row, column = lax.axis_index("ty"), lax.axis_index("tx")
    up, down = row * 16 + column + 16, row * 16 + column - 16
    chip = jnp.where(flip == 1, down, up)
    beyond = jnp.where(flip == 1, up, down)
    left = row * 16 + lax.rem(column + 15, 16)
    right = row * 16 + lax.rem(column + 1, 16)
    tile = (row * 16 + column, chip, beyond, left, right)
    lane128 = lanes((128, 128))
    sub128 = lax.broadcasted_iota(i32, (128, 128), 0)
    select = jnp.zeros((128, 128), f32)
    for t in range(5):
        select = jnp.where((lane128 == t) & (sub128 == tile[t]), 1.0, select)
    columns = dot(count[...].astype(f32).astype(bf16), select.astype(bf16))
    below = (lane128 < sub128).astype(f32).astype(bf16)
    first = dot(below, columns.astype(bf16))

    masks = [
        sea[...].astype(f32),
        chip_in[0, pl.ds(BINS, 4), :],
        z_in[0, pl.ds(BINS, 4), :],
        left_in[0, pl.ds(40, 4), :],
        right_in[0, pl.ds(40, 4), :],
    ]
    stacked = jnp.concatenate(masks + [jnp.zeros((4, 128), f32)], 0)
    upto = (sub128 <= lane128).astype(f32).astype(bf16)
    prefix = dot(stacked.astype(bf16), upto)
    ranks = []
    for t in range(5):
        before = jnp.zeros((1, 1), f32)
        for r in range(4):
            line = prefix[4 * t + r : 4 * t + r + 1]
            ranks.append(jnp.where(masks[t][r : r + 1] > 0.5, line - 1.0 + before, -2.0))
            before = before + line[:, 127:128]

    def flipped(t, j, table):
        return jnp.where(flip == 1, table[4 * t + 3 - j], table[4 * t + j])

    mask_rows = [masks[t][r : r + 1] for t in range(5) for r in range(4)]
    own_rank = [flipped(0, j, ranks) for j in range(4)]
    own_mask = [flipped(0, j, mask_rows) for j in range(4)]
    chip_rank = [flipped(1, j, ranks) for j in range(2)]
    chip_mask = [flipped(1, j, mask_rows) for j in range(2)]
    z_rank = [flipped(2, 3 - j, ranks) for j in range(2)]
    z_mask = [flipped(2, 3 - j, mask_rows) for j in range(2)]
    left_rank = pack_edges([flipped(3, j, ranks) for j in range(4)])[0:1]
    right_rank = pack_edges([flipped(4, j, ranks) for j in range(4)])[0:1]
    left_mask = pack_edges([flipped(3, j, mask_rows) for j in range(4)])
    right_mask = pack_edges([flipped(4, j, mask_rows) for j in range(4)])

    turned = jnp.transpose(arrived[...])
    values = split3(jnp.concatenate([turned[16 * s : 16 * s + 16] for s in range(4)], 1))

    keys = []
    for t in range(5):
        number, start = columns[:, t : t + 1], first[:, t : t + 1]
        keys.append(
            jnp.concatenate([jnp.where(number > s, start + s, -1.0) for s in range(4)], 0)
        )

    def place(t, rank):
        chosen = (keys[t] == rank).astype(f32).astype(bf16)
        found = dot(values, chosen)
        return found[:16] + found[16:32] + found[32:]

    own = [place(0, own_rank[j]) for j in range(4)]
    near_chip = [place(1, chip_rank[j]) for j in range(2)]
    near_z = [place(2, z_rank[j]) for j in range(2)]
    found_left, found_right = place(3, left_rank), place(4, right_rank)

    def pick(found, chip_side, k):
        use_up = (flip == 0) if chip_side else (flip == 1)
        return jnp.where(use_up, found[5 + k : 6 + k], found[7 + k : 8 + k])

    def stack(rows):
        return jnp.concatenate(rows, 0)

    v8 = stack([pick(near_z[1], False, 0), pick(near_z[0], False, 0)] + [o[1:2] for o in own] + [pick(near_chip[0], True, 0), pick(near_chip[1], True, 0)])
    h8 = stack([pick(near_z[1], False, 1), pick(near_z[0], False, 1)] + [o[2:3] for o in own] + [pick(near_chip[0], True, 1), pick(near_chip[1], True, 1)])
    m8 = stack([z_mask[1], z_mask[0]] + own_mask + [chip_mask[0], chip_mask[1]])
    zero4 = jnp.zeros((4, 128), f32)
    own_m = stack(own_mask + [zero4])
    own_u = stack([o[0:1] for o in own] + [zero4])
    own_sx = stack([o[3:4] for o in own] + [zero4])
    own_sy = stack([o[4:5] for o in own] + [zero4])
    sign = jnp.where(flip == 1, -1.0, 1.0).astype(f32)
    water[...] = own_m
    depth8 = jnp.where(m8 > 0.5, h8, land_depth)
    m8s = m8 * courant_scale
    own_ms = own_m * courant_scale
    ux[...] = faces(own_u * own_ms, own_m, 1)
    vy[...] = roll(faces(v8 * m8s, m8, 0), -1, 0) * sign
    turn_x = own_sx * own_m * (0.5 * turn_scale)
    turn_y = own_sy * own_m * (0.5 * turn_scale)

    def one(f, carry):
        speed, turning = kinematics(depth8, jnp.broadcast_to(sigma_rows[pl.ds(f, 1), :], (8, 128)))
        cgy[f] = roll(faces(speed * m8s, m8, 0), -1, 0) * sign
        cgx[f] = faces(roll(speed, -2, 0) * own_ms, own_m, 1)
        turning = roll(turning, -2, 0)
        tx[f] = turning * turn_x
        ty[f] = turning * turn_y
        return carry

    lax.fori_loop(0, NF, one, 0, unroll=4)

    low = lanes() % 8 < 4
    own_mask_edge = pack_edges(own_mask)
    own_u_edge = pack_edges([o[0:1] for o in own])
    own_h_edge = pack_edges([o[2:3] for o in own])
    for side in range(2):
        outside = low if side == 0 else jnp.logical_not(low)
        found = found_left[9:11] if side == 0 else found_right[11:13]
        mask = jnp.where(outside, left_mask if side == 0 else right_mask, own_mask_edge)
        u = jnp.where(outside, found[0:1], own_u_edge)
        h = jnp.where(outside, found[1:2], own_h_edge)
        depth = jnp.where(mask > 0.5, h, land_depth)
        edge_u[side] = faces(u * (mask * courant_scale), mask, 1)
        for part in range(2):
            speed, _ = kinematics(depth, sigma_packed[pl.ds(8 * part, 8), :])
            edge_cg[side, pl.ds(8 * part, 8), :] = faces(speed * (mask * courant_scale), mask, 1)


def flux(speed, behind, ahead):
    return speed * jnp.where(speed > 0.0, behind, ahead)


def through_east(value, speed):
    third = 1.0 / 3.0
    return flux(speed, value - roll(value, 1) * third, roll(value, -1) - roll(value, -2) * third)


def step_kernel(high, make_fix, pack, last, halo, na, nb, *refs):
    refs = list(refs)
    take = lambda n: [refs.pop(0) for _ in range(n)]
    if make_fix:
        edges, left_in, right_in = take(3)
    else:
        (fix,) = take(1)
    cgx, cgy, tx, ty, ux, vy, water, edge_cg, edge_u, cosine, sine = take(11)
    other = take(1)[0] if pack or last else None
    out = take(1)[0]
    if make_fix:
        (fix,) = take(1)
    if pack:
        out_edges, to_east, to_west = take(3)
    edge_halo, edge_flux, east, moved, turn, swirl, buffer, done = refs
    flip = parity()
    lane = lanes()
    low = lane % 8 < 4
    first = 2 if high else 0
    own = nb if high else na

    def edge_group(g, carry):
        for b, start in enumerate(STARTS):
            c = cosine[pl.ds(start, 8), :]
            for side in range(2):
                speed = c * edge_cg[side, pl.ds(g, 1), :] + edge_u[side]
                here = pl.ds(8 * b, 8)
                edge_flux[side, g, here, :] = through_east(edge_halo[side, g, here, :], speed)
        return carry

    def x_group(g, carry):
        for q in range(4):
            f = 4 * g + q
            for start in STARTS:
                here = pl.ds(f * ND + start, 8)
                c = cosine[pl.ds(start, 8), :]
                for j in range(2):
                    speed = c * cgx[f, pl.ds(first + j, 1), :] + ux[pl.ds(first + j, 1), :]
                    east[j, here, :] = through_east(own[j, here, :], speed)
        return carry

    def fix_group(g, carry):
        for b in range(5):
            here = pl.ds(8 * b, 8)
            left, right = edge_flux[0, g, here, :], edge_flux[1, g, here, :]
            fix[g, here, :] = jnp.where(low, right - roll(right, 1), left - roll(left, 1))
        return carry

    if make_fix:
        unpack_sends(edges, left_in, right_in, edge_halo)
        lax.fori_loop(0, GROUPS, edge_group, 0)
    x_group(0, 0)
    if make_fix:
        lax.fori_loop(0, GROUPS, fix_group, 0)
    at_edge = (lane < 2) | (lane >= 126)

    def one(g, q):
        f = 4 * g + q
        for b, start in enumerate(STARTS):
            base = f * ND + start
            c, s = cosine[pl.ds(start, 8), :], sine[pl.ds(start, 8), :]
            here = pl.ds(base, 8)
            value = [na[0, here, :], na[1, here, :], nb[0, here, :], nb[1, here, :]]
            if high:
                value = value + [halo[1, here, :], halo[0, here, :]]
            else:
                value = [halo[1, here, :], halo[0, here, :]] + value
            third = [v * (1.0 / 3.0) for v in value]
            across = []
            for k in range(3):
                speed = s * cgy[f, pl.ds(first + k, 1), :] + vy[pl.ds(first + k, 1), :]
                across.append(flux(speed, value[k + 1] - third[k], value[k + 2] - third[k + 3]))
            edge = fix[g, pl.ds(8 * b, 8), :]
            for j in range(2):
                row = first + j
                through = east[j, here, :]
                change = jnp.where(at_edge, roll(edge, -(32 * q + 8 * row + 4)), through - roll(through, 1))
                moved[q, j, pl.ds(8 + start, 8), :] = value[j + 2] - change - (across[j + 1] - across[j])
                half = s * tx[f, pl.ds(row, 1), :] - c * ty[f, pl.ds(row, 1), :]
                turn[q, j, pl.ds(8 + start, 8), :] = jnp.clip(half, -0.5 * refraction_limit, 0.5 * refraction_limit)
        for j in range(2):
            moved[q, j, pl.ds(8 + ND, 1), :] = moved[q, j, pl.ds(8, 1), :]
            turn[q, j, pl.ds(8 + ND, 1), :] = turn[q, j, pl.ds(8, 1), :]
            for start in STARTS:
                speed = turn[q, j, pl.ds(8 + start, 8), :] + turn[q, j, pl.ds(9 + start, 8), :]
                swirl[q, j, pl.ds(8 + start, 8), :] = flux(
                    speed, moved[q, j, pl.ds(8 + start, 8), :], moved[q, j, pl.ds(9 + start, 8), :]
                )
            swirl[q, j, pl.ds(7, 1), :] = swirl[q, j, pl.ds(7 + ND, 1), :]

    def finish(g, q, start):
        base = (4 * g + q) * ND + start
        for j in range(2):
            value = (
                moved[q, j, pl.ds(8 + start, 8), :]
                - swirl[q, j, pl.ds(8 + start, 8), :]
                + swirl[q, j, pl.ds(7 + start, 8), :]
            ) * water[pl.ds(first + j, 1), :]
            if last:
                buffer[pl.ds(4 * base + jnp.where(flip == 1, 3 - j, j), 8, stride=4), :] = value
                buffer[pl.ds(4 * base + jnp.where(flip == 1, 1 - j, 2 + j), 8, stride=4), :] = other[j, pl.ds(base, 8), :]
            else:
                out[j, pl.ds(base, 8), :] = value

    def result(g):
        rows = pl.ds(pl.multiple_of(576 * g, 8), 576)
        return pltpu.make_async_copy(buffer.at[rows, :], out.at[rows, :], done.at[g])

    def group(g, carry):
        for q in range(4):
            one(g, q)
        for q in range(4):
            for start in STARTS:
                finish(g, q, start)
        if last:
            result(g).start()
        x_group(jnp.minimum(g + 1, GROUPS - 1), 0)
        return carry

    lax.fori_loop(0, GROUPS, group, 0)
    if last:
        for g in range(GROUPS):
            result(g).wait()
    if pack:
        pack_planes(other, out, out_edges)
        pack_sends(out_edges, to_east, to_west)


def shape(*dims, dtype=f32):
    return jax.ShapeDtypeStruct(dims, dtype)


def call(kernel, out, scratch=(), limit=8, cost=2_000_000, moved=4_000_000, **specs):
    return pl.pallas_call(
        kernel,
        out_shape=out,
        scratch_shapes=list(scratch),
        compiler_params=pltpu.CompilerParams(vmem_limit_bytes=limit << 20),
        cost_estimate=pl.CostEstimate(flops=cost, bytes_accessed=moved, transcendentals=0),
        **specs,
    )


PLANE = shape(2, ROWS, 128)
EDGES = shape(GROUPS, 40, 128)
SENDS = shape(3, 48, 128)


def step(high, make_fix, pack, last, *operands):
    out = [shape(4 * BINS, 128) if last else PLANE]
    specs = {}
    if make_fix:
        out.append(shape(GROUPS, 40, 128))
    if pack:
        out += [EDGES, SENDS, SENDS]
    if last:
        specs["out_specs"] = [pl.BlockSpec(memory_space=pltpu.MemorySpace.HBM)]
    scratch = [
        pltpu.VMEM((2, GROUPS, 40, 128) if make_fix else (8, 128), f32),
        pltpu.VMEM((2, GROUPS, 40, 128) if make_fix else (8, 128), f32),
        pltpu.VMEM((2, BINS, 128), f32),
        pltpu.VMEM((4, 2, 56, 128), f32),
        pltpu.VMEM((4, 2, 56, 128), f32),
        pltpu.VMEM((4, 2, 56, 128), f32),
        pltpu.VMEM((4 * BINS, 128) if last else (8, 128), f32),
        pltpu.SemaphoreType.DMA((GROUPS,)),
    ]
    return call(functools.partial(step_kernel, high, make_fix, pack, last), out, scratch, 8, **specs)(*operands)


Z_PAIRS = [p for z in range(3) for p in ((2 * z + 1, 2 * z + 2), (2 * z + 2, 2 * z + 1))]
CHIP_PAIRS = [p for z in range(4) for p in ((2 * z, 2 * z + 1), (2 * z + 1, 2 * z))]


def swap_z(rows):
    return lax.ppermute(rows, "ty", Z_PAIRS)


def swap_chip(rows):
    return lax.ppermute(rows, "ty", CHIP_PAIRS)


def swap_x(to_east, to_west):
    east = [(i, (i + 1) % 16) for i in range(16)]
    west = [((i + 1) % 16, i) for i in range(16)]
    return lax.ppermute(to_east, "tx", east), lax.ppermute(to_west, "tx", west)


def on_device(spectra, sea_mask, currents, sea_depth, slopes, piece_offset, piece_count):
    flat = spectra.reshape(4 * BINS, 128)
    pieces = call(pieces_kernel, shape(128, 128), [pltpu.VMEM((128, 128), f32)], 60)(
        currents, sea_depth.reshape(1, 1024), slopes, piece_offset, piece_count
    )
    pieces, sea_mask = lax.optimization_barrier((pieces, sea_mask))
    na, nb, edges, to_east, to_west = call(planes_kernel, (PLANE, PLANE, EDGES, SENDS, SENDS), limit=8)(flat, sea_mask)
    z_in = swap_z(na)
    chip_in = swap_chip(nb)
    left_in, right_in = swap_x(to_east, to_west)
    arrived = lax.all_to_all(pieces, ("ty", "tx"), split_axis=0, concat_axis=0, tiled=True)
    per_frequency = shape(NF, 8, 128)
    speeds = call(
        fields_kernel, (per_frequency,) * 4 + (shape(8, 128),) * 3 + (shape(2, 16, 128), shape(2, 8, 128)), limit=12
    )(arrived, piece_count, sea_mask, chip_in, z_in, left_in, right_in, SIGMA_ROWS, SIGMA_PACKED)
    common = (*speeds, COSINE, SINE)
    new_a, fix = step(False, True, False, False, z_in, na, nb, edges, left_in, right_in, *common)
    z_in = swap_z(new_a)
    new_b, edges, to_east, to_west = step(True, False, True, False, chip_in, na, nb, fix, *common, new_a)
    chip_in = swap_chip(new_b)
    left_in, right_in = swap_x(to_east, to_west)
    end_b, fix = step(True, True, False, False, chip_in, new_a, new_b, edges, left_in, right_in, *common)
    (out,) = step(False, False, False, True, z_in, new_a, new_b, fix, *common, end_b)
    return out.reshape(spectra.shape)


def solution(mesh):
    return jax.shard_map(
        on_device,
        mesh=mesh,
        in_specs=(
            P(None, None, "ty", "tx"),
            P("ty", "tx"),
            P(None, ("ty", "tx")),
            P(("ty", "tx")),
            P(None, ("ty", "tx")),
            P(),
            P(),
        ),
        out_specs=P(None, None, "ty", "tx"),
        check_vma=False,
    )
```

```python
import functools
import math

import jax
import jax.numpy as jnp
import numpy as np
from jax import lax
from jax.experimental import pallas as pl
from jax.experimental.pallas import tpu as pltpu
from jax.sharding import PartitionSpec as P


NF, ND = 36, 36
BINS = NF * ND
ROWS = BINS + 8
GROUPS = NF // 4
STARTS = (0, 8, 16, 24, 28)

gravity = 9.81
first_frequency = 0.0418
frequency_ratio = 1.1
time_step = 600.0
cell_metres = 13900.0
refraction_limit = 0.8
land_depth = 1000.0
product_limit = 20.0
courant_scale = time_step / cell_metres
turn_scale = time_step * ND / (2.0 * math.pi)

f32, bf16, i32 = jnp.float32, jnp.bfloat16, jnp.int32
HEADING = np.arange(48) % ND * (2.0 * math.pi / ND)
COSINE = np.broadcast_to(np.cos(HEADING)[:, None], (48, 128)).astype(np.float32)
SINE = np.broadcast_to(np.sin(HEADING)[:, None], (48, 128)).astype(np.float32)
SIGMA = (2.0 * math.pi * first_frequency * frequency_ratio ** np.arange(64)).astype(np.float32)
SIGMA_ROWS = np.broadcast_to(SIGMA[:NF, None], (NF, 128)).astype(np.float32)
SIGMA_PACKED = np.where(
    np.arange(16)[:, None] < GROUPS, SIGMA[np.minimum(4 * np.arange(16)[:, None] + np.arange(128)[None, :] // 32, 35)], 1.0
).astype(np.float32)


def roll(x, shift, axis=1):
    size = x.shape[axis]
    if isinstance(shift, int):
        shift %= size
        return x if shift == 0 else pltpu.roll(x, shift, axis)
    return pltpu.roll(x, shift, axis)


def lanes(shape=(8, 128)):
    return lax.broadcasted_iota(i32, shape, len(shape) - 1)


def split3(x):
    high = x.astype(bf16)
    rest = x - high.astype(f32)
    middle = rest.astype(bf16)
    low = (rest - middle.astype(f32)).astype(bf16)
    return jnp.concatenate([high, middle, low], 0)


def dot(a, b):
    return jnp.dot(a, b, preferred_element_type=f32)


def parity():
    return lax.rem(lax.axis_index("ty"), 2)


def prepare_kernel(
    source_ref, sea, currents, depth, slopes, offset, count,
    na_out, nb_out, edges, to_east, to_west, pieces,
    rows, spectra, na, nb, arrived, sent,
):
    def fetch(g):
        part = pl.ds(pl.multiple_of(576 * g, 8), 576)
        return pltpu.make_async_copy(source_ref.at[part, :], spectra.at[part, :], arrived.at[g])

    def send(half, g):
        part = pl.ds(pl.multiple_of(144 * g, 8), 144)
        held, out = ((na, na_out), (nb, nb_out))[half]
        return pltpu.make_async_copy(held.at[:, part, :], out.at[:, part, :], sent.at[half, g])

    def send_tail(half):
        held, out = ((na, na_out), (nb, nb_out))[half]
        return pltpu.make_async_copy(
            held.at[:, pl.ds(BINS, 8), :], out.at[:, pl.ds(BINS, 8), :], sent.at[half, GROUPS]
        )

    for g in range(GROUPS):
        fetch(g).start()
    pieces_kernel(currents, depth, slopes, offset, count, pieces, rows)
    flip = parity()
    mask = sea[...].astype(f32)
    tail = jnp.concatenate([mask, jnp.zeros((4, 128), f32)], 0)
    for part in range(2):
        na[part, pl.ds(BINS, 8), :] = tail
        nb[part, pl.ds(BINS, 8), :] = tail
    send_tail(0).start()
    send_tail(1).start()
    to_east[0, pl.ds(40, 8), :] = tail
    to_west[0, pl.ds(40, 8), :] = tail
    row_mask = [jnp.broadcast_to(jnp.where(flip == 1, mask[3 - j : 4 - j], mask[j : j + 1]), (8, 128)) for j in range(4)]
    source = [jnp.where(flip == 1, 3 - j, j) for j in range(4)]

    def group(g, carry):
        fetch(g).wait()
        for k in range(18):
            base = 144 * g + 8 * k
            for j in range(4):
                (na if j < 2 else nb)[j % 2, pl.ds(base, 8), :] = (
                    spectra[pl.ds(4 * base + source[j], 8, stride=4), :] * row_mask[j]
                )
        send(0, g).start()
        send(1, g).start()
        return carry

    lax.fori_loop(0, GROUPS, group, 0)
    pack_planes(na, nb, edges)
    pack_sends(edges, to_east, to_west)
    for half in range(2):
        send_tail(half).wait()
        for g in range(GROUPS):
            send(half, g).wait()


def pack_planes(na, nb, edges):
    lane = lanes()

    def group(g, carry):
        for b, start in enumerate(STARTS):
            packed = jnp.zeros((8, 128), f32)
            for q in range(4):
                for j in range(4):
                    value = (na if j < 2 else nb)[j % 2, pl.ds((4 * g + q) * ND + start, 8), :]
                    at = 32 * q + 8 * j
                    packed = jnp.where((lane >= at) & (lane < at + 8), roll(value, at + 4), packed)
            edges[g, pl.ds(8 * b, 8), :] = packed
        return carry

    lax.fori_loop(0, GROUPS, group, 0)


SHIFTS = (0, 2, 4, -2)


def place_of(first, g):
    return lanes() % 8 // 2 == (first + SHIFTS[g % 4]) % 8 // 2


def pack_sends(edges, to_east, to_west):
    for b in range(5):
        here = pl.ds(8 * b, 8)
        for first in range(0, GROUPS, 4):
            east, west = jnp.zeros((8, 128), f32), jnp.zeros((8, 128), f32)
            for g in range(first, min(first + 4, GROUPS)):
                value = roll(edges[g, here, :], SHIFTS[g % 4])
                east = jnp.where(place_of(2, g), value, east)
                west = jnp.where(place_of(4, g), value, west)
            to_east[first // 4, here, :] = east
            to_west[first // 4, here, :] = west


def unpack_sends(edges, left_in, right_in, halo):
    c = lanes() % 8 // 2
    for b in range(5):
        here = pl.ds(8 * b, 8)
        for g in range(GROUPS):
            mine = edges[g, here, :]
            halo[0, g, here, :] = jnp.where(c == 1, roll(left_in[g // 4, here, :], -SHIFTS[g % 4]), mine)
            halo[1, g, here, :] = jnp.where(c == 2, roll(right_in[g // 4, here, :], -SHIFTS[g % 4]), mine)


def pieces_kernel(currents, depth, slopes, offset, count, out, rows):
    me = lax.axis_index("ty") * 16 + lax.axis_index("tx")
    table = jnp.concatenate([currents[...], depth[...], slopes[...], jnp.zeros((3, 1024), f32)], 0)
    shifted = jnp.concatenate([roll(table, -s) for s in range(4)], 0)
    wanted = offset[pl.ds(me, 1), :]
    number = count[pl.ds(me, 1), :]
    chosen = (lax.broadcasted_iota(i32, (1024, 128), 0) == wanted).astype(f32).astype(bf16)
    picked = dot(split3(shifted), chosen)
    picked = picked[:32] + picked[32:64] + picked[64:]
    lane = lanes()
    for s in range(4):
        own = jnp.where(number > s, picked[8 * s : 8 * s + 8], 0.0)
        up, down = roll(own, -16), roll(own, 16)
        left = jnp.where(lane % 16 == 0, roll(own, -15), roll(own, 1))
        right = jnp.where(lane % 16 == 15, roll(own, 15), roll(own, -1))
        rows[pl.ds(16 * s, 16), :] = jnp.concatenate(
            [own[:5], up[1:3], down[1:3], left[0:1], left[2:3], right[0:1], right[2:3], jnp.zeros((3, 128), f32)], 0
        )
    rows[pl.ds(64, 64), :] = jnp.zeros((64, 128), f32)
    out[...] = jnp.transpose(rows[...])


def kinematics(water_depth, sigma):
    squared = sigma * sigma
    initial = squared / (gravity * jnp.sqrt(jnp.tanh(squared * water_depth / gravity)))
    hyperbolic = jnp.tanh(initial * water_depth)
    residue = gravity * initial * hyperbolic - squared
    derivative = gravity * hyperbolic + gravity * initial * water_depth * (1.0 - hyperbolic * hyperbolic)
    wavenumber = initial - residue / derivative
    product = jnp.minimum(wavenumber * water_depth, product_limit)
    growth = jnp.exp(2.0 * product)
    double = 0.5 * (growth - 1.0 / growth)
    return sigma / wavenumber * (0.5 + product / double), sigma / double


def pack_edges(rows):
    lane = lanes()
    total = jnp.zeros((8, 128), f32)
    for j, row in enumerate(rows):
        wide = jnp.broadcast_to(row, (8, 128))
        for at in range(8 * j, 128, 32):
            total = jnp.where((lane >= at) & (lane < at + 8), roll(wide, at + 4), total)
    return total


def faces(x, mask, axis):
    ahead = roll(x, -1, axis)
    value = (9.0 * (x + ahead) - roll(x, 1, axis) - roll(x, -2, axis)) * (1.5 / 16.0)
    return value * (mask * roll(mask, -1, axis))


def fields_kernel(
    arrived, count, sea, chip_in, z_in, left_in, right_in, sigma_rows, sigma_packed,
    cgx, cgy, tx, ty, ux, vy, water, edge_cg, edge_u,
):
    flip = parity()
    row, column = lax.axis_index("ty"), lax.axis_index("tx")
    up, down = row * 16 + column + 16, row * 16 + column - 16
    chip = jnp.where(flip == 1, down, up)
    beyond = jnp.where(flip == 1, up, down)
    left = row * 16 + lax.rem(column + 15, 16)
    right = row * 16 + lax.rem(column + 1, 16)
    tile = (row * 16 + column, chip, beyond, left, right)
    lane128 = lanes((128, 128))
    sub128 = lax.broadcasted_iota(i32, (128, 128), 0)
    select = jnp.zeros((128, 128), f32)
    for t in range(5):
        select = jnp.where((lane128 == t) & (sub128 == tile[t]), 1.0, select)
    columns = dot(count[...].astype(f32).astype(bf16), select.astype(bf16))
    below = (lane128 < sub128).astype(f32).astype(bf16)
    first = dot(below, columns.astype(bf16))

    masks = [
        sea[...].astype(f32),
        chip_in[0, pl.ds(BINS, 4), :],
        z_in[0, pl.ds(BINS, 4), :],
        left_in[0, pl.ds(40, 4), :],
        right_in[0, pl.ds(40, 4), :],
    ]
    stacked = jnp.concatenate(masks + [jnp.zeros((4, 128), f32)], 0)
    upto = (sub128 <= lane128).astype(f32).astype(bf16)
    prefix = dot(stacked.astype(bf16), upto)
    ranks = []
    for t in range(5):
        before = jnp.zeros((1, 1), f32)
        for r in range(4):
            line = prefix[4 * t + r : 4 * t + r + 1]
            ranks.append(jnp.where(masks[t][r : r + 1] > 0.5, line - 1.0 + before, -2.0))
            before = before + line[:, 127:128]

    def flipped(t, j, table):
        return jnp.where(flip == 1, table[4 * t + 3 - j], table[4 * t + j])

    mask_rows = [masks[t][r : r + 1] for t in range(5) for r in range(4)]
    own_rank = [flipped(0, j, ranks) for j in range(4)]
    own_mask = [flipped(0, j, mask_rows) for j in range(4)]
    chip_rank = [flipped(1, j, ranks) for j in range(2)]
    chip_mask = [flipped(1, j, mask_rows) for j in range(2)]
    z_rank = [flipped(2, 3 - j, ranks) for j in range(2)]
    z_mask = [flipped(2, 3 - j, mask_rows) for j in range(2)]
    left_rank = pack_edges([flipped(3, j, ranks) for j in range(4)])[0:1]
    right_rank = pack_edges([flipped(4, j, ranks) for j in range(4)])[0:1]
    left_mask = pack_edges([flipped(3, j, mask_rows) for j in range(4)])
    right_mask = pack_edges([flipped(4, j, mask_rows) for j in range(4)])

    turned = jnp.transpose(arrived[...])
    values = split3(jnp.concatenate([turned[16 * s : 16 * s + 16] for s in range(4)], 1))

    keys = []
    for t in range(5):
        number, start = columns[:, t : t + 1], first[:, t : t + 1]
        keys.append(
            jnp.concatenate([jnp.where(number > s, start + s, -1.0) for s in range(4)], 0)
        )

    def place(t, rank):
        chosen = (keys[t] == rank).astype(f32).astype(bf16)
        found = dot(values, chosen)
        return found[:16] + found[16:32] + found[32:]

    own = [place(0, own_rank[j]) for j in range(4)]
    near_chip = [place(1, chip_rank[j]) for j in range(2)]
    near_z = [place(2, z_rank[j]) for j in range(2)]
    found_left, found_right = place(3, left_rank), place(4, right_rank)

    def pick(found, chip_side, k):
        use_up = (flip == 0) if chip_side else (flip == 1)
        return jnp.where(use_up, found[5 + k : 6 + k], found[7 + k : 8 + k])

    def stack(rows):
        return jnp.concatenate(rows, 0)

    v8 = stack([pick(near_z[1], False, 0), pick(near_z[0], False, 0)] + [o[1:2] for o in own] + [pick(near_chip[0], True, 0), pick(near_chip[1], True, 0)])
    h8 = stack([pick(near_z[1], False, 1), pick(near_z[0], False, 1)] + [o[2:3] for o in own] + [pick(near_chip[0], True, 1), pick(near_chip[1], True, 1)])
    m8 = stack([z_mask[1], z_mask[0]] + own_mask + [chip_mask[0], chip_mask[1]])
    zero4 = jnp.zeros((4, 128), f32)
    own_m = stack(own_mask + [zero4])
    own_u = stack([o[0:1] for o in own] + [zero4])
    own_sx = stack([o[3:4] for o in own] + [zero4])
    own_sy = stack([o[4:5] for o in own] + [zero4])
    sign = jnp.where(flip == 1, -1.0, 1.0).astype(f32)
    water[...] = own_m
    depth8 = jnp.where(m8 > 0.5, h8, land_depth)
    m8s = m8 * courant_scale
    own_ms = own_m * courant_scale
    ux[...] = faces(own_u * own_ms, own_m, 1)
    vy[...] = roll(faces(v8 * m8s, m8, 0), -1, 0) * sign
    turn_x = own_sx * own_m * (0.5 * turn_scale)
    turn_y = own_sy * own_m * (0.5 * turn_scale)

    def one(f, carry):
        speed, turning = kinematics(depth8, jnp.broadcast_to(sigma_rows[pl.ds(f, 1), :], (8, 128)))
        cgy[f] = roll(faces(speed * m8s, m8, 0), -1, 0) * sign
        cgx[f] = faces(roll(speed, -2, 0) * own_ms, own_m, 1)
        turning = roll(turning, -2, 0)
        tx[f] = turning * turn_x
        ty[f] = turning * turn_y
        return carry

    lax.fori_loop(0, NF, one, 0, unroll=4)

    low = lanes() % 8 < 4
    own_mask_edge = pack_edges(own_mask)
    own_u_edge = pack_edges([o[0:1] for o in own])
    own_h_edge = pack_edges([o[2:3] for o in own])
    for side in range(2):
        outside = low if side == 0 else jnp.logical_not(low)
        found = found_left[9:11] if side == 0 else found_right[11:13]
        mask = jnp.where(outside, left_mask if side == 0 else right_mask, own_mask_edge)
        u = jnp.where(outside, found[0:1], own_u_edge)
        h = jnp.where(outside, found[1:2], own_h_edge)
        depth = jnp.where(mask > 0.5, h, land_depth)
        edge_u[side] = faces(u * (mask * courant_scale), mask, 1)
        for part in range(2):
            speed, _ = kinematics(depth, sigma_packed[pl.ds(8 * part, 8), :])
            edge_cg[side, pl.ds(8 * part, 8), :] = faces(speed * (mask * courant_scale), mask, 1)


def flux(speed, behind, ahead):
    return speed * jnp.where(speed > 0.0, behind, ahead)


def through_east(value, speed):
    third = 1.0 / 3.0
    return flux(speed, value - roll(value, 1) * third, roll(value, -1) - roll(value, -2) * third)


def step_kernel(high, make_fix, pack, last, halo, na, nb, *refs):
    refs = list(refs)
    take = lambda n: [refs.pop(0) for _ in range(n)]
    if make_fix:
        edges, left_in, right_in = take(3)
    else:
        (fix,) = take(1)
    cgx, cgy, tx, ty, ux, vy, water, edge_cg, edge_u, cosine, sine = take(11)
    other = take(1)[0] if pack or last else None
    out = take(1)[0]
    if make_fix:
        (fix,) = take(1)
    if pack:
        out_edges, to_east, to_west = take(3)
    edge_halo, edge_flux, east, moved, turn, swirl, buffer, done = refs
    flip = parity()
    lane = lanes()
    low = lane % 8 < 4
    first = 2 if high else 0
    own = nb if high else na

    def edge_group(g, carry):
        for b, start in enumerate(STARTS):
            c = cosine[pl.ds(start, 8), :]
            for side in range(2):
                speed = c * edge_cg[side, pl.ds(g, 1), :] + edge_u[side]
                here = pl.ds(8 * b, 8)
                edge_flux[side, g, here, :] = through_east(edge_halo[side, g, here, :], speed)
        return carry

    def x_group(g, carry):
        for q in range(4):
            f = 4 * g + q
            for start in STARTS:
                here = pl.ds(f * ND + start, 8)
                c = cosine[pl.ds(start, 8), :]
                for j in range(2):
                    speed = c * cgx[f, pl.ds(first + j, 1), :] + ux[pl.ds(first + j, 1), :]
                    east[j, here, :] = through_east(own[j, here, :], speed)
        return carry

    def fix_group(g, carry):
        for b in range(5):
            here = pl.ds(8 * b, 8)
            left, right = edge_flux[0, g, here, :], edge_flux[1, g, here, :]
            fix[g, here, :] = jnp.where(low, right - roll(right, 1), left - roll(left, 1))
        return carry

    if make_fix:
        unpack_sends(edges, left_in, right_in, edge_halo)
        lax.fori_loop(0, GROUPS, edge_group, 0)
    x_group(0, 0)
    if make_fix:
        lax.fori_loop(0, GROUPS, fix_group, 0)
    at_edge = (lane < 2) | (lane >= 126)

    def one(g, q):
        f = 4 * g + q
        for b, start in enumerate(STARTS):
            base = f * ND + start
            c, s = cosine[pl.ds(start, 8), :], sine[pl.ds(start, 8), :]
            here = pl.ds(base, 8)
            value = [na[0, here, :], na[1, here, :], nb[0, here, :], nb[1, here, :]]
            if high:
                value = value + [halo[1, here, :], halo[0, here, :]]
            else:
                value = [halo[1, here, :], halo[0, here, :]] + value
            third = [v * (1.0 / 3.0) for v in value]
            across = []
            for k in range(3):
                speed = s * cgy[f, pl.ds(first + k, 1), :] + vy[pl.ds(first + k, 1), :]
                across.append(flux(speed, value[k + 1] - third[k], value[k + 2] - third[k + 3]))
            edge = fix[g, pl.ds(8 * b, 8), :]
            for j in range(2):
                row = first + j
                through = east[j, here, :]
                change = jnp.where(at_edge, roll(edge, -(32 * q + 8 * row + 4)), through - roll(through, 1))
                moved[q, j, pl.ds(8 + start, 8), :] = value[j + 2] - change - (across[j + 1] - across[j])
                half = s * tx[f, pl.ds(row, 1), :] - c * ty[f, pl.ds(row, 1), :]
                turn[q, j, pl.ds(8 + start, 8), :] = jnp.clip(half, -0.5 * refraction_limit, 0.5 * refraction_limit)
        for j in range(2):
            moved[q, j, pl.ds(8 + ND, 1), :] = moved[q, j, pl.ds(8, 1), :]
            turn[q, j, pl.ds(8 + ND, 1), :] = turn[q, j, pl.ds(8, 1), :]
            for start in STARTS:
                speed = turn[q, j, pl.ds(8 + start, 8), :] + turn[q, j, pl.ds(9 + start, 8), :]
                swirl[q, j, pl.ds(8 + start, 8), :] = flux(
                    speed, moved[q, j, pl.ds(8 + start, 8), :], moved[q, j, pl.ds(9 + start, 8), :]
                )
            swirl[q, j, pl.ds(7, 1), :] = swirl[q, j, pl.ds(7 + ND, 1), :]

    def finish(g, q, start):
        base = (4 * g + q) * ND + start
        for j in range(2):
            value = (
                moved[q, j, pl.ds(8 + start, 8), :]
                - swirl[q, j, pl.ds(8 + start, 8), :]
                + swirl[q, j, pl.ds(7 + start, 8), :]
            ) * water[pl.ds(first + j, 1), :]
            if last:
                buffer[pl.ds(4 * base + jnp.where(flip == 1, 3 - j, j), 8, stride=4), :] = value
                buffer[pl.ds(4 * base + jnp.where(flip == 1, 1 - j, 2 + j), 8, stride=4), :] = other[j, pl.ds(base, 8), :]
            else:
                out[j, pl.ds(base, 8), :] = value

    def result(g):
        rows = pl.ds(pl.multiple_of(576 * g, 8), 576)
        return pltpu.make_async_copy(buffer.at[rows, :], out.at[rows, :], done.at[g])

    def group(g, carry):
        for q in range(4):
            one(g, q)
        for q in range(4):
            for start in STARTS:
                finish(g, q, start)
        if last:
            result(g).start()
        x_group(jnp.minimum(g + 1, GROUPS - 1), 0)
        return carry

    lax.fori_loop(0, GROUPS, group, 0)
    if last:
        for g in range(GROUPS):
            result(g).wait()
    if pack:
        pack_planes(other, out, out_edges)
        pack_sends(out_edges, to_east, to_west)


def shape(*dims, dtype=f32):
    return jax.ShapeDtypeStruct(dims, dtype)


def call(kernel, out, scratch=(), limit=8, cost=2_000_000, moved=4_000_000, **specs):
    return pl.pallas_call(
        kernel,
        out_shape=out,
        scratch_shapes=list(scratch),
        compiler_params=pltpu.CompilerParams(vmem_limit_bytes=limit << 20),
        cost_estimate=pl.CostEstimate(flops=cost, bytes_accessed=moved, transcendentals=0),
        **specs,
    )


PLANE = shape(2, ROWS, 128)
EDGES = shape(GROUPS, 40, 128)
SENDS = shape(3, 48, 128)


def step(high, make_fix, pack, last, *operands):
    out = [shape(4 * BINS, 128) if last else PLANE]
    specs = {}
    if make_fix:
        out.append(shape(GROUPS, 40, 128))
    if pack:
        out += [EDGES, SENDS, SENDS]
    if last:
        specs["out_specs"] = [pl.BlockSpec(memory_space=pltpu.MemorySpace.HBM)]
    scratch = [
        pltpu.VMEM((2, GROUPS, 40, 128) if make_fix else (8, 128), f32),
        pltpu.VMEM((2, GROUPS, 40, 128) if make_fix else (8, 128), f32),
        pltpu.VMEM((2, BINS, 128), f32),
        pltpu.VMEM((4, 2, 56, 128), f32),
        pltpu.VMEM((4, 2, 56, 128), f32),
        pltpu.VMEM((4, 2, 56, 128), f32),
        pltpu.VMEM((4 * BINS, 128) if last else (8, 128), f32),
        pltpu.SemaphoreType.DMA((GROUPS,)),
    ]
    return call(functools.partial(step_kernel, high, make_fix, pack, last), out, scratch, 8, **specs)(*operands)


Z_PAIRS = [p for z in range(3) for p in ((2 * z + 1, 2 * z + 2), (2 * z + 2, 2 * z + 1))]
CHIP_PAIRS = [p for z in range(4) for p in ((2 * z, 2 * z + 1), (2 * z + 1, 2 * z))]


def swap_z(rows):
    return lax.ppermute(rows, "ty", Z_PAIRS)


def swap_chip(rows):
    return lax.ppermute(rows, "ty", CHIP_PAIRS)


def swap_x(to_east, to_west):
    east = [(i, (i + 1) % 16) for i in range(16)]
    west = [((i + 1) % 16, i) for i in range(16)]
    return lax.ppermute(to_east, "tx", east), lax.ppermute(to_west, "tx", west)


def on_device(spectra, sea_mask, currents, sea_depth, slopes, piece_offset, piece_count):
    flat = spectra.reshape(4 * BINS, 128)
    hbm, vmem = (pl.BlockSpec(memory_space=kind) for kind in (pltpu.MemorySpace.HBM, pltpu.MemorySpace.VMEM))
    na, nb, edges, to_east, to_west, pieces = call(
        prepare_kernel,
        (PLANE, PLANE, EDGES, SENDS, SENDS, shape(128, 128)),
        [
            pltpu.VMEM((128, 128), f32),
            pltpu.VMEM((4 * BINS, 128), f32),
            pltpu.VMEM(PLANE.shape, f32),
            pltpu.VMEM(PLANE.shape, f32),
            pltpu.SemaphoreType.DMA((GROUPS,)),
            pltpu.SemaphoreType.DMA((2, GROUPS + 1)),
        ],
        60,
        in_specs=[hbm] + [vmem] * 6,
        out_specs=[hbm] * 2 + [vmem] * 4,
    )(flat, sea_mask, currents, sea_depth.reshape(1, 1024), slopes, piece_offset, piece_count)
    z_in = swap_z(na)
    chip_in = swap_chip(nb)
    left_in, right_in = swap_x(to_east, to_west)
    arrived = lax.all_to_all(pieces, ("ty", "tx"), split_axis=0, concat_axis=0, tiled=True)
    per_frequency = shape(NF, 8, 128)
    speeds = call(
        fields_kernel, (per_frequency,) * 4 + (shape(8, 128),) * 3 + (shape(2, 16, 128), shape(2, 8, 128)), limit=12
    )(arrived, piece_count, sea_mask, chip_in, z_in, left_in, right_in, SIGMA_ROWS, SIGMA_PACKED)
    common = (*speeds, COSINE, SINE)
    new_a, fix = step(False, True, False, False, z_in, na, nb, edges, left_in, right_in, *common)
    z_in = swap_z(new_a)
    new_b, edges, to_east, to_west = step(True, False, True, False, chip_in, na, nb, fix, *common, new_a)
    chip_in = swap_chip(new_b)
    left_in, right_in = swap_x(to_east, to_west)
    end_b, fix = step(True, True, False, False, chip_in, new_a, new_b, edges, left_in, right_in, *common)
    (out,) = step(False, False, False, True, z_in, new_a, new_b, fix, *common, end_b)
    return out.reshape(spectra.shape)


def solution(mesh):
    return jax.shard_map(
        on_device,
        mesh=mesh,
        in_specs=(
            P(None, None, "ty", "tx"),
            P("ty", "tx"),
            P(None, ("ty", "tx")),
            P(("ty", "tx")),
            P(None, ("ty", "tx")),
            P(),
            P(),
        ),
        out_specs=P(None, None, "ty", "tx"),
        check_vma=False,
    )
```

```python
import functools
import math

import jax
import jax.numpy as jnp
import numpy as np
from jax import lax
from jax.experimental import pallas as pl
from jax.experimental.pallas import tpu as pltpu
from jax.sharding import PartitionSpec as P


NF, ND = 36, 36
BINS = NF * ND
ROWS = BINS + 8
GROUPS = NF // 4
STARTS = (0, 8, 16, 24, 28)

gravity = 9.81
first_frequency = 0.0418
frequency_ratio = 1.1
time_step = 600.0
cell_metres = 13900.0
refraction_limit = 0.8
land_depth = 1000.0
product_limit = 20.0
courant_scale = time_step / cell_metres
turn_scale = time_step * ND / (2.0 * math.pi)

f32, bf16, i32 = jnp.float32, jnp.bfloat16, jnp.int32
HEADING = np.arange(48) % ND * (2.0 * math.pi / ND)
COSINE = np.broadcast_to(np.cos(HEADING)[:, None], (48, 128)).astype(np.float32)
SINE = np.broadcast_to(np.sin(HEADING)[:, None], (48, 128)).astype(np.float32)
AT = np.arange(128)


def shift_matrix(ahead):
    return (AT[:, None] == (AT[None, :] + ahead) % 128).astype(np.float32)


STENCIL = np.concatenate([3.0 * shift_matrix(0) - shift_matrix(-1), 3.0 * shift_matrix(1) - shift_matrix(2)], 1)
STENCIL = np.concatenate([STENCIL, STENCIL], 0).astype(jnp.bfloat16)
SIGMA = (2.0 * math.pi * first_frequency * frequency_ratio ** np.arange(64)).astype(np.float32)
SIGMA_ROWS = np.broadcast_to(SIGMA[:NF, None], (NF, 128)).astype(np.float32)
SIGMA_PACKED = np.where(
    np.arange(16)[:, None] < GROUPS, SIGMA[np.minimum(4 * np.arange(16)[:, None] + np.arange(128)[None, :] // 32, 35)], 1.0
).astype(np.float32)


def roll(x, shift, axis=1):
    size = x.shape[axis]
    if isinstance(shift, int):
        shift %= size
        return x if shift == 0 else pltpu.roll(x, shift, axis)
    return pltpu.roll(x, shift, axis)


def lanes(shape=(8, 128)):
    return lax.broadcasted_iota(i32, shape, len(shape) - 1)


def split3(x):
    high = x.astype(bf16)
    rest = x - high.astype(f32)
    middle = rest.astype(bf16)
    low = (rest - middle.astype(f32)).astype(bf16)
    return jnp.concatenate([high, middle, low], 0)


def dot(a, b):
    return jnp.dot(a, b, preferred_element_type=f32)


def parity():
    return lax.rem(lax.axis_index("ty"), 2)


def prepare_kernel(
    source_ref, sea, currents, depth, slopes, offset, count,
    na_out, nb_out, edges, to_east, to_west, pieces,
    rows, spectra, na, nb, arrived, sent,
):
    def fetch(g):
        part = pl.ds(pl.multiple_of(576 * g, 8), 576)
        return pltpu.make_async_copy(source_ref.at[part, :], spectra.at[part, :], arrived.at[g])

    def send(half, g):
        part = pl.ds(pl.multiple_of(144 * g, 8), 144)
        held, out = ((na, na_out), (nb, nb_out))[half]
        return pltpu.make_async_copy(held.at[:, part, :], out.at[:, part, :], sent.at[half, g])

    def send_tail(half):
        held, out = ((na, na_out), (nb, nb_out))[half]
        return pltpu.make_async_copy(
            held.at[:, pl.ds(BINS, 8), :], out.at[:, pl.ds(BINS, 8), :], sent.at[half, GROUPS]
        )

    for g in range(GROUPS):
        fetch(g).start()
    pieces_kernel(currents, depth, slopes, offset, count, pieces, rows)
    flip = parity()
    mask = sea[...].astype(f32)
    tail = jnp.concatenate([mask, jnp.zeros((4, 128), f32)], 0)
    for part in range(2):
        na[part, pl.ds(BINS, 8), :] = tail
        nb[part, pl.ds(BINS, 8), :] = tail
    send_tail(0).start()
    send_tail(1).start()
    to_east[0, pl.ds(40, 8), :] = tail
    to_west[0, pl.ds(40, 8), :] = tail
    row_mask = [jnp.broadcast_to(jnp.where(flip == 1, mask[3 - j : 4 - j], mask[j : j + 1]), (8, 128)) for j in range(4)]
    source = [jnp.where(flip == 1, 3 - j, j) for j in range(4)]

    def group(g, carry):
        fetch(g).wait()
        for k in range(18):
            base = 144 * g + 8 * k
            for j in range(4):
                (na if j < 2 else nb)[j % 2, pl.ds(base, 8), :] = (
                    spectra[pl.ds(4 * base + source[j], 8, stride=4), :] * row_mask[j]
                )
        send(0, g).start()
        send(1, g).start()
        pack_group(na, nb, edges, jnp.maximum(g - 1, 0))
        return carry

    lax.fori_loop(0, GROUPS, group, 0)
    pack_group(na, nb, edges, GROUPS - 1)
    pack_sends(edges, to_east, to_west)
    for half in range(2):
        send_tail(half).wait()
        for g in range(GROUPS):
            send(half, g).wait()


def pack_group(na, nb, edges, g):
    lane = lanes()
    for b, start in enumerate(STARTS):
        packed = None
        for q in reversed(range(4)):
            for j in reversed(range(4)):
                value = (na if j < 2 else nb)[j % 2, pl.ds((4 * g + q) * ND + start, 8), :]
                at = 32 * q + 8 * j
                value = roll(value, at + 4)
                packed = value if packed is None else jnp.where(lane < at + 8, value, packed)
        edges[g, pl.ds(8 * b, 8), :] = packed


SHIFTS = (0, 2, 4, -2)


def place_of(first, g):
    return lanes() % 8 // 2 == (first + SHIFTS[g % 4]) % 8 // 2


def pack_sends(edges, to_east, to_west):
    for b in range(5):
        here = pl.ds(8 * b, 8)
        for first in range(0, GROUPS, 4):
            east, west = jnp.zeros((8, 128), f32), jnp.zeros((8, 128), f32)
            for g in range(first, min(first + 4, GROUPS)):
                value = roll(edges[g, here, :], SHIFTS[g % 4])
                east = jnp.where(place_of(2, g), value, east)
                west = jnp.where(place_of(4, g), value, west)
            to_east[first // 4, here, :] = east
            to_west[first // 4, here, :] = west


def unpack_sends(edges, left_in, right_in, halo):
    c = lanes() % 8 // 2
    for b in range(5):
        here = pl.ds(8 * b, 8)
        for g in range(GROUPS):
            mine = edges[g, here, :]
            halo[0, g, here, :] = jnp.where(c == 1, roll(left_in[g // 4, here, :], -SHIFTS[g % 4]), mine)
            halo[1, g, here, :] = jnp.where(c == 2, roll(right_in[g // 4, here, :], -SHIFTS[g % 4]), mine)


def pieces_kernel(currents, depth, slopes, offset, count, out, rows):
    me = lax.axis_index("ty") * 16 + lax.axis_index("tx")
    table = jnp.concatenate([currents[...], depth[...], slopes[...], jnp.zeros((3, 1024), f32)], 0)
    shifted = jnp.concatenate([roll(table, -s) for s in range(4)], 0)
    wanted = offset[pl.ds(me, 1), :]
    number = count[pl.ds(me, 1), :]
    chosen = (lax.broadcasted_iota(i32, (1024, 128), 0) == wanted).astype(f32).astype(bf16)
    picked = dot(split3(shifted), chosen)
    picked = picked[:32] + picked[32:64] + picked[64:]
    lane = lanes()
    for s in range(4):
        own = jnp.where(number > s, picked[8 * s : 8 * s + 8], 0.0)
        up, down = roll(own, -16), roll(own, 16)
        left = jnp.where(lane % 16 == 0, roll(own, -15), roll(own, 1))
        right = jnp.where(lane % 16 == 15, roll(own, 15), roll(own, -1))
        rows[pl.ds(16 * s, 16), :] = jnp.concatenate(
            [own[:5], up[1:3], down[1:3], left[0:1], left[2:3], right[0:1], right[2:3], jnp.zeros((3, 128), f32)], 0
        )
    rows[pl.ds(64, 64), :] = jnp.zeros((64, 128), f32)
    out[...] = jnp.transpose(rows[...])


def kinematics(water_depth, sigma):
    squared = sigma * sigma
    initial = squared / (gravity * jnp.sqrt(jnp.tanh(squared * water_depth / gravity)))
    hyperbolic = jnp.tanh(initial * water_depth)
    residue = gravity * initial * hyperbolic - squared
    derivative = gravity * hyperbolic + gravity * initial * water_depth * (1.0 - hyperbolic * hyperbolic)
    wavenumber = initial - residue / derivative
    product = jnp.minimum(wavenumber * water_depth, product_limit)
    growth = jnp.exp(2.0 * product)
    double = 0.5 * (growth - 1.0 / growth)
    return sigma / wavenumber * (0.5 + product / double), sigma / double


def pack_edges(rows):
    lane = lanes()
    total = jnp.zeros((8, 128), f32)
    for j, row in enumerate(rows):
        wide = jnp.broadcast_to(row, (8, 128))
        for at in range(8 * j, 128, 32):
            total = jnp.where((lane >= at) & (lane < at + 8), roll(wide, at + 4), total)
    return total


def faces(x, mask, axis):
    ahead = roll(x, -1, axis)
    value = (9.0 * (x + ahead) - roll(x, 1, axis) - roll(x, -2, axis)) * (0.5 / 16.0)
    return value * (mask * roll(mask, -1, axis))


def fields_kernel(
    arrived, count, sea, chip_in, z_in, left_in, right_in, sigma_rows, sigma_packed,
    cgx, cgy, tx, ty, ux, vy, water, edge_cg, edge_u,
):
    flip = parity()
    row, column = lax.axis_index("ty"), lax.axis_index("tx")
    up, down = row * 16 + column + 16, row * 16 + column - 16
    chip = jnp.where(flip == 1, down, up)
    beyond = jnp.where(flip == 1, up, down)
    left = row * 16 + lax.rem(column + 15, 16)
    right = row * 16 + lax.rem(column + 1, 16)
    tile = (row * 16 + column, chip, beyond, left, right)
    lane128 = lanes((128, 128))
    sub128 = lax.broadcasted_iota(i32, (128, 128), 0)
    select = jnp.zeros((128, 128), f32)
    for t in range(5):
        select = jnp.where((lane128 == t) & (sub128 == tile[t]), 1.0, select)
    columns = dot(count[...].astype(f32).astype(bf16), select.astype(bf16))
    below = (lane128 < sub128).astype(f32).astype(bf16)
    first = dot(below, columns.astype(bf16))

    masks = [
        sea[...].astype(f32),
        chip_in[0, pl.ds(BINS, 4), :],
        z_in[0, pl.ds(BINS, 4), :],
        left_in[0, pl.ds(40, 4), :],
        right_in[0, pl.ds(40, 4), :],
    ]
    stacked = jnp.concatenate(masks + [jnp.zeros((4, 128), f32)], 0)
    upto = (sub128 <= lane128).astype(f32).astype(bf16)
    prefix = dot(stacked.astype(bf16), upto)
    ranks = []
    for t in range(5):
        before = jnp.zeros((1, 1), f32)
        for r in range(4):
            line = prefix[4 * t + r : 4 * t + r + 1]
            ranks.append(jnp.where(masks[t][r : r + 1] > 0.5, line - 1.0 + before, -2.0))
            before = before + line[:, 127:128]

    def flipped(t, j, table):
        return jnp.where(flip == 1, table[4 * t + 3 - j], table[4 * t + j])

    mask_rows = [masks[t][r : r + 1] for t in range(5) for r in range(4)]
    own_rank = [flipped(0, j, ranks) for j in range(4)]
    own_mask = [flipped(0, j, mask_rows) for j in range(4)]
    chip_rank = [flipped(1, j, ranks) for j in range(2)]
    chip_mask = [flipped(1, j, mask_rows) for j in range(2)]
    z_rank = [flipped(2, 3 - j, ranks) for j in range(2)]
    z_mask = [flipped(2, 3 - j, mask_rows) for j in range(2)]
    left_rank = pack_edges([flipped(3, j, ranks) for j in range(4)])[0:1]
    right_rank = pack_edges([flipped(4, j, ranks) for j in range(4)])[0:1]
    left_mask = pack_edges([flipped(3, j, mask_rows) for j in range(4)])
    right_mask = pack_edges([flipped(4, j, mask_rows) for j in range(4)])

    turned = jnp.transpose(arrived[...])
    values = split3(jnp.concatenate([turned[16 * s : 16 * s + 16] for s in range(4)], 1))

    keys = []
    for t in range(5):
        number, start = columns[:, t : t + 1], first[:, t : t + 1]
        keys.append(
            jnp.concatenate([jnp.where(number > s, start + s, -1.0) for s in range(4)], 0)
        )

    def place(t, rank):
        chosen = (keys[t] == rank).astype(f32).astype(bf16)
        found = dot(values, chosen)
        return found[:16] + found[16:32] + found[32:]

    own = [place(0, own_rank[j]) for j in range(4)]
    near_chip = [place(1, chip_rank[j]) for j in range(2)]
    near_z = [place(2, z_rank[j]) for j in range(2)]
    found_left, found_right = place(3, left_rank), place(4, right_rank)

    def pick(found, chip_side, k):
        use_up = (flip == 0) if chip_side else (flip == 1)
        return jnp.where(use_up, found[5 + k : 6 + k], found[7 + k : 8 + k])

    def stack(rows):
        return jnp.concatenate(rows, 0)

    v8 = stack([pick(near_z[1], False, 0), pick(near_z[0], False, 0)] + [o[1:2] for o in own] + [pick(near_chip[0], True, 0), pick(near_chip[1], True, 0)])
    h8 = stack([pick(near_z[1], False, 1), pick(near_z[0], False, 1)] + [o[2:3] for o in own] + [pick(near_chip[0], True, 1), pick(near_chip[1], True, 1)])
    m8 = stack([z_mask[1], z_mask[0]] + own_mask + [chip_mask[0], chip_mask[1]])
    zero4 = jnp.zeros((4, 128), f32)
    own_m = stack(own_mask + [zero4])
    own_u = stack([o[0:1] for o in own] + [zero4])
    own_sx = stack([o[3:4] for o in own] + [zero4])
    own_sy = stack([o[4:5] for o in own] + [zero4])
    sign = jnp.where(flip == 1, -1.0, 1.0).astype(f32)
    water[...] = own_m
    depth8 = jnp.where(m8 > 0.5, h8, land_depth)
    m8s = m8 * courant_scale
    own_ms = own_m * courant_scale
    ux[...] = faces(own_u * own_ms, own_m, 1)
    vy[...] = roll(faces(v8 * m8s, m8, 0), -1, 0) * sign
    turn_x = own_sx * own_m * (0.5 * turn_scale)
    turn_y = own_sy * own_m * (0.5 * turn_scale)

    def one(f, carry):
        speed, turning = kinematics(depth8, jnp.broadcast_to(sigma_rows[pl.ds(f, 1), :], (8, 128)))
        cgy[f] = roll(faces(speed * m8s, m8, 0), -1, 0) * sign
        cgx[f] = faces(roll(speed, -2, 0) * own_ms, own_m, 1)
        turning = roll(turning, -2, 0)
        tx[f] = turning * turn_x
        ty[f] = turning * turn_y
        return carry

    lax.fori_loop(0, NF, one, 0, unroll=4)

    low = lanes() % 8 < 4
    own_mask_edge = pack_edges(own_mask)
    own_u_edge = pack_edges([o[0:1] for o in own])
    own_h_edge = pack_edges([o[2:3] for o in own])
    for side in range(2):
        outside = low if side == 0 else jnp.logical_not(low)
        found = found_left[9:11] if side == 0 else found_right[11:13]
        mask = jnp.where(outside, left_mask if side == 0 else right_mask, own_mask_edge)
        u = jnp.where(outside, found[0:1], own_u_edge)
        h = jnp.where(outside, found[1:2], own_h_edge)
        depth = jnp.where(mask > 0.5, h, land_depth)
        edge_u[side] = faces(u * (mask * courant_scale), mask, 1)
        for part in range(2):
            speed, _ = kinematics(depth, sigma_packed[pl.ds(8 * part, 8), :])
            edge_cg[side, pl.ds(8 * part, 8), :] = faces(speed * (mask * courant_scale), mask, 1)


def flux(speed, behind, ahead):
    return speed * jnp.where(speed > 0.0, behind, ahead)


def through_east(value, speed):
    triple = 3.0 * value
    return flux(speed, triple - roll(value, 1), roll(triple, -1) - roll(value, -2))


def step_kernel(high, make_fix, pack, last, again, halo, na, nb, *refs):
    refs = list(refs)
    take = lambda n: [refs.pop(0) for _ in range(n)]
    if make_fix:
        edges, left_in, right_in = take(3)
    else:
        (fix,) = take(1)
    cgx, cgy, tx, ty, ux, vy, water, edge_cg, edge_u, cosine, sine, stencil = take(12)
    other = take(1)[0] if pack or last else None
    if again:
        east_speed, north_speed, turn_speed = take(3)
    out = take(1)[0]
    if make_fix:
        (fix,) = take(1)
    if pack:
        out_edges, to_east, to_west = take(3)
    if not again:
        east_speed, north_speed, turn_speed = take(3)
    edge_halo, edge_flux, east, moved, turn, swirl, buffer, done = refs
    flip = parity()
    lane = lanes()
    low = lane % 8 < 4
    first = 2 if high else 0
    own = nb if high else na

    def edge_group(g, carry):
        for b, start in enumerate(STARTS):
            c = cosine[pl.ds(start, 8), :]
            for side in range(2):
                speed = c * edge_cg[side, pl.ds(g, 1), :] + edge_u[side]
                here = pl.ds(8 * b, 8)
                edge_flux[side, g, here, :] = through_east(edge_halo[side, g, here, :], speed)
        return carry

    def x_group(g, carry):
        places = [(q, start, j) for q in range(4) for start in STARTS for j in range(2)]
        value = jnp.concatenate([own[j, pl.ds((4 * g + q) * ND + start, 8), :] for q, start, j in places], 0)
        upper = value.astype(bf16)
        lower = (value - upper.astype(f32)).astype(bf16)
        sides = dot(jnp.concatenate([upper, lower], 1), stencil[...])
        for r, (q, start, j) in enumerate(places):
            f = 4 * g + q
            here = pl.ds(f * ND + start, 8)
            if again:
                speed = east_speed[j, here, :]
            else:
                c = cosine[pl.ds(start, 8), :]
                speed = c * cgx[f, pl.ds(first + j, 1), :] + ux[pl.ds(first + j, 1), :]
                east_speed[j, here, :] = speed
            both = sides[8 * r : 8 * r + 8]
            east[j, here, :] = flux(speed, both[:, :128], both[:, 128:])
        return carry

    def fix_group(g, carry):
        for b in range(5):
            here = pl.ds(8 * b, 8)
            left, right = edge_flux[0, g, here, :], edge_flux[1, g, here, :]
            fix[g, here, :] = jnp.where(low, right - roll(right, 1), left - roll(left, 1))
        return carry

    if make_fix:
        unpack_sends(edges, left_in, right_in, edge_halo)
        lax.fori_loop(0, GROUPS, edge_group, 0)
    x_group(0, 0)
    if make_fix:
        lax.fori_loop(0, GROUPS, fix_group, 0)
    at_edge = (lane < 2) | (lane >= 126)

    def one(g, q):
        f = 4 * g + q
        for b, start in enumerate(STARTS):
            base = f * ND + start
            c, s = cosine[pl.ds(start, 8), :], sine[pl.ds(start, 8), :]
            here = pl.ds(base, 8)
            value = [na[0, here, :], na[1, here, :], nb[0, here, :], nb[1, here, :]]
            if high:
                value = value + [halo[1, here, :], halo[0, here, :]]
            else:
                value = [halo[1, here, :], halo[0, here, :]] + value
            triple = [3.0 * v for v in value]
            across = []
            for k in range(3):
                if again:
                    speed = north_speed[k, here, :]
                else:
                    speed = s * cgy[f, pl.ds(first + k, 1), :] + vy[pl.ds(first + k, 1), :]
                    north_speed[k, here, :] = speed
                across.append(flux(speed, triple[k + 1] - value[k], triple[k + 2] - value[k + 3]))
            edge = fix[g, pl.ds(8 * b, 8), :]
            for j in range(2):
                row = first + j
                through = east[j, here, :]
                change = jnp.where(at_edge, roll(edge, -(32 * q + 8 * row + 4)), through - roll(through, 1))
                moved[q, j, pl.ds(8 + start, 8), :] = value[j + 2] - change - (across[j + 1] - across[j])
                if again:
                    continue
                half = s * tx[f, pl.ds(row, 1), :] - c * ty[f, pl.ds(row, 1), :]
                turn[q, j, pl.ds(8 + start, 8), :] = jnp.clip(half, -0.5 * refraction_limit, 0.5 * refraction_limit)
        for j in range(2):
            moved[q, j, pl.ds(8 + ND, 1), :] = moved[q, j, pl.ds(8, 1), :]
            if not again:
                turn[q, j, pl.ds(8 + ND, 1), :] = turn[q, j, pl.ds(8, 1), :]
            for start in STARTS:
                here = pl.ds((4 * g + q) * ND + start, 8)
                if again:
                    speed = turn_speed[j, here, :]
                else:
                    speed = turn[q, j, pl.ds(8 + start, 8), :] + turn[q, j, pl.ds(9 + start, 8), :]
                    turn_speed[j, here, :] = speed
                swirl[q, j, pl.ds(8 + start, 8), :] = flux(
                    speed, moved[q, j, pl.ds(8 + start, 8), :], moved[q, j, pl.ds(9 + start, 8), :]
                )
            swirl[q, j, pl.ds(7, 1), :] = swirl[q, j, pl.ds(7 + ND, 1), :]

    def finish(g, q, start):
        base = (4 * g + q) * ND + start
        for j in range(2):
            value = (
                moved[q, j, pl.ds(8 + start, 8), :]
                - swirl[q, j, pl.ds(8 + start, 8), :]
                + swirl[q, j, pl.ds(7 + start, 8), :]
            ) * water[pl.ds(first + j, 1), :]
            if last:
                buffer[pl.ds(4 * base + jnp.where(flip == 1, 3 - j, j), 8, stride=4), :] = value
                buffer[pl.ds(4 * base + jnp.where(flip == 1, 1 - j, 2 + j), 8, stride=4), :] = other[j, pl.ds(base, 8), :]
            else:
                out[j, pl.ds(base, 8), :] = value

    def result(g):
        rows = pl.ds(pl.multiple_of(576 * g, 8), 576)
        return pltpu.make_async_copy(buffer.at[rows, :], out.at[rows, :], done.at[g])

    def group(g, carry):
        for q in range(4):
            one(g, q)
        for q in range(4):
            for start in STARTS:
                finish(g, q, start)
        if last:
            result(g).start()
        x_group(jnp.minimum(g + 1, GROUPS - 1), 0)
        if pack:
            pack_group(other, out, out_edges, jnp.maximum(g - 1, 0))
        return carry

    lax.fori_loop(0, GROUPS, group, 0)
    if last:
        for g in range(GROUPS):
            result(g).wait()
    if pack:
        pack_group(other, out, out_edges, GROUPS - 1)
        pack_sends(out_edges, to_east, to_west)


def shape(*dims, dtype=f32):
    return jax.ShapeDtypeStruct(dims, dtype)


def call(kernel, out, scratch=(), limit=8, cost=2_000_000, moved=4_000_000, **specs):
    return pl.pallas_call(
        kernel,
        out_shape=out,
        scratch_shapes=list(scratch),
        compiler_params=pltpu.CompilerParams(vmem_limit_bytes=limit << 20),
        cost_estimate=pl.CostEstimate(flops=cost, bytes_accessed=moved, transcendentals=0),
        **specs,
    )


PLANE = shape(2, ROWS, 128)
EDGES = shape(GROUPS, 40, 128)
SENDS = shape(3, 48, 128)


def step(high, make_fix, pack, last, again, *operands):
    out = [shape(4 * BINS, 128) if last else PLANE]
    specs = {}
    if make_fix:
        out.append(shape(GROUPS, 40, 128))
    if pack:
        out += [EDGES, SENDS, SENDS]
    if not again:
        out += [shape(2, BINS, 128), shape(3, BINS, 128), shape(2, BINS, 128)]
    if last:
        specs["out_specs"] = [pl.BlockSpec(memory_space=pltpu.MemorySpace.HBM)]
    scratch = [
        pltpu.VMEM((2, GROUPS, 40, 128) if make_fix else (8, 128), f32),
        pltpu.VMEM((2, GROUPS, 40, 128) if make_fix else (8, 128), f32),
        pltpu.VMEM((2, BINS, 128), f32),
        pltpu.VMEM((4, 2, 56, 128), f32),
        pltpu.VMEM((4, 2, 56, 128), f32),
        pltpu.VMEM((4, 2, 56, 128), f32),
        pltpu.VMEM((4 * BINS, 128) if last else (8, 128), f32),
        pltpu.SemaphoreType.DMA((GROUPS,)),
    ]
    return call(functools.partial(step_kernel, high, make_fix, pack, last, again), out, scratch, 8, **specs)(*operands)


Z_PAIRS = [p for z in range(3) for p in ((2 * z + 1, 2 * z + 2), (2 * z + 2, 2 * z + 1))]
CHIP_PAIRS = [p for z in range(4) for p in ((2 * z, 2 * z + 1), (2 * z + 1, 2 * z))]


def swap_z(rows):
    return lax.ppermute(rows, "ty", Z_PAIRS)


def swap_chip(rows):
    return lax.ppermute(rows, "ty", CHIP_PAIRS)


def swap_x(to_east, to_west):
    east = [(i, (i + 1) % 16) for i in range(16)]
    west = [((i + 1) % 16, i) for i in range(16)]
    return lax.ppermute(to_east, "tx", east), lax.ppermute(to_west, "tx", west)


def on_device(spectra, sea_mask, currents, sea_depth, slopes, piece_offset, piece_count):
    flat = spectra.reshape(4 * BINS, 128)
    hbm, vmem = (pl.BlockSpec(memory_space=kind) for kind in (pltpu.MemorySpace.HBM, pltpu.MemorySpace.VMEM))
    na, nb, edges, to_east, to_west, pieces = call(
        prepare_kernel,
        (PLANE, PLANE, EDGES, SENDS, SENDS, shape(128, 128)),
        [
            pltpu.VMEM((128, 128), f32),
            pltpu.VMEM((4 * BINS, 128), f32),
            pltpu.VMEM(PLANE.shape, f32),
            pltpu.VMEM(PLANE.shape, f32),
            pltpu.SemaphoreType.DMA((GROUPS,)),
            pltpu.SemaphoreType.DMA((2, GROUPS + 1)),
        ],
        60,
        in_specs=[hbm] + [vmem] * 6,
        out_specs=[hbm] * 2 + [vmem] * 4,
    )(flat, sea_mask, currents, sea_depth.reshape(1, 1024), slopes, piece_offset, piece_count)
    z_in = swap_z(na)
    chip_in = swap_chip(nb)
    left_in, right_in = swap_x(to_east, to_west)
    arrived = lax.all_to_all(pieces, ("ty", "tx"), split_axis=0, concat_axis=0, tiled=True)
    per_frequency = shape(NF, 8, 128)
    speeds = call(
        fields_kernel, (per_frequency,) * 4 + (shape(8, 128),) * 3 + (shape(2, 16, 128), shape(2, 8, 128)), limit=12
    )(arrived, piece_count, sea_mask, chip_in, z_in, left_in, right_in, SIGMA_ROWS, SIGMA_PACKED)
    common = (*speeds, COSINE, SINE, STENCIL)
    new_a, fix, *low_speeds = step(False, True, False, False, False, z_in, na, nb, edges, left_in, right_in, *common)
    z_in = swap_z(new_a)
    new_b, edges, to_east, to_west, *high_speeds = step(True, False, True, False, False, chip_in, na, nb, fix, *common, new_a)
    chip_in = swap_chip(new_b)
    left_in, right_in = swap_x(to_east, to_west)
    end_b, fix = step(
        True, True, False, False, True, chip_in, new_a, new_b, edges, left_in, right_in, *common, *high_speeds
    )
    (out,) = step(False, False, False, True, True, z_in, new_a, new_b, fix, *common, end_b, *low_speeds)
    return out.reshape(spectra.shape)


def solution(mesh):
    return jax.shard_map(
        on_device,
        mesh=mesh,
        in_specs=(
            P(None, None, "ty", "tx"),
            P("ty", "tx"),
            P(None, ("ty", "tx")),
            P(("ty", "tx")),
            P(None, ("ty", "tx")),
            P(),
            P(),
        ),
        out_specs=P(None, None, "ty", "tx"),
        check_vma=False,
    )
```

```python
import functools
import math

import jax
import jax.numpy as jnp
import numpy as np
from jax import lax
from jax.experimental import pallas as pl
from jax.experimental.pallas import tpu as pltpu
from jax.sharding import PartitionSpec as P


NF, ND = 36, 36
BINS = NF * ND
ROWS = BINS + 8
GROUPS = NF // 4
STARTS = (0, 8, 16, 24, 28)

gravity = 9.81
first_frequency = 0.0418
frequency_ratio = 1.1
time_step = 600.0
cell_metres = 13900.0
refraction_limit = 0.8
land_depth = 1000.0
product_limit = 20.0
courant_scale = time_step / cell_metres
turn_scale = time_step * ND / (2.0 * math.pi)

f32, bf16, i32 = jnp.float32, jnp.bfloat16, jnp.int32
HEADING = np.arange(48) % ND * (2.0 * math.pi / ND)
COSINE = np.broadcast_to(np.cos(HEADING)[:, None], (48, 128)).astype(np.float32)
SINE = np.broadcast_to(np.sin(HEADING)[:, None], (48, 128)).astype(np.float32)
AT = np.arange(128)


def shift_matrix(ahead):
    return (AT[:, None] == (AT[None, :] + ahead) % 128).astype(np.float32)


STENCIL = np.concatenate([3.0 * shift_matrix(0) - shift_matrix(-1), 3.0 * shift_matrix(1) - shift_matrix(2)], 1)
STENCIL = np.concatenate([STENCIL, STENCIL], 0).astype(jnp.bfloat16)
SIGMA = (2.0 * math.pi * first_frequency * frequency_ratio ** np.arange(64)).astype(np.float32)
SIGMA_ROWS = np.broadcast_to(SIGMA[:NF, None], (NF, 128)).astype(np.float32)
SIGMA_PACKED = np.where(
    np.arange(16)[:, None] < GROUPS, SIGMA[np.minimum(4 * np.arange(16)[:, None] + np.arange(128)[None, :] // 32, 35)], 1.0
).astype(np.float32)


def roll(x, shift, axis=1):
    size = x.shape[axis]
    if isinstance(shift, int):
        shift %= size
        return x if shift == 0 else pltpu.roll(x, shift, axis)
    return pltpu.roll(x, shift, axis)


def lanes(shape=(8, 128)):
    return lax.broadcasted_iota(i32, shape, len(shape) - 1)


def split3(x):
    high = x.astype(bf16)
    rest = x - high.astype(f32)
    middle = rest.astype(bf16)
    low = (rest - middle.astype(f32)).astype(bf16)
    return jnp.concatenate([high, middle, low], 0)


def dot(a, b):
    return jnp.dot(a, b, preferred_element_type=f32)


def parity():
    return lax.rem(lax.axis_index("ty"), 2)


def prepare_kernel(
    source_ref, sea, currents, depth, slopes, offset, count,
    na_out, nb_out, edges, to_east, to_west, pieces,
    rows, spectra, na, nb, arrived, sent,
):
    def fetch(g):
        part = pl.ds(pl.multiple_of(576 * g, 8), 576)
        return pltpu.make_async_copy(source_ref.at[part, :], spectra.at[part, :], arrived.at[g])

    def send(half, g):
        part = pl.ds(pl.multiple_of(144 * g, 8), 144)
        held, out = ((na, na_out), (nb, nb_out))[half]
        return pltpu.make_async_copy(held.at[:, part, :], out.at[:, part, :], sent.at[half, g])

    def send_tail(half):
        held, out = ((na, na_out), (nb, nb_out))[half]
        return pltpu.make_async_copy(
            held.at[:, pl.ds(BINS, 8), :], out.at[:, pl.ds(BINS, 8), :], sent.at[half, GROUPS]
        )

    for g in range(GROUPS):
        fetch(g).start()
    pieces_kernel(currents, depth, slopes, offset, count, pieces, rows)
    flip = parity()
    mask = sea[...].astype(f32)
    tail = jnp.concatenate([mask, jnp.zeros((4, 128), f32)], 0)
    for part in range(2):
        na[part, pl.ds(BINS, 8), :] = tail
        nb[part, pl.ds(BINS, 8), :] = tail
    send_tail(0).start()
    send_tail(1).start()
    to_east[0, pl.ds(40, 8), :] = tail
    to_west[0, pl.ds(40, 8), :] = tail
    row_mask = [jnp.broadcast_to(jnp.where(flip == 1, mask[3 - j : 4 - j], mask[j : j + 1]), (8, 128)) for j in range(4)]
    source = [jnp.where(flip == 1, 3 - j, j) for j in range(4)]

    def group(g, carry):
        fetch(g).wait()
        for k in range(18):
            base = 144 * g + 8 * k
            for j in range(4):
                (na if j < 2 else nb)[j % 2, pl.ds(base, 8), :] = (
                    spectra[pl.ds(4 * base + source[j], 8, stride=4), :] * row_mask[j]
                )
        send(0, g).start()
        send(1, g).start()
        pack_group(na, nb, edges, jnp.maximum(g - 1, 0))
        return carry

    lax.fori_loop(0, GROUPS, group, 0)
    pack_group(na, nb, edges, GROUPS - 1)
    pack_sends(edges, to_east, to_west)
    for half in range(2):
        send_tail(half).wait()
        for g in range(GROUPS):
            send(half, g).wait()


def pack_group(na, nb, edges, g):
    lane = lanes()
    for b, start in enumerate(STARTS):
        packed = None
        for q in reversed(range(4)):
            for j in reversed(range(4)):
                value = (na if j < 2 else nb)[j % 2, pl.ds((4 * g + q) * ND + start, 8), :]
                at = 32 * q + 8 * j
                value = roll(value, at + 4)
                packed = value if packed is None else jnp.where(lane < at + 8, value, packed)
        edges[g, pl.ds(8 * b, 8), :] = packed


SHIFTS = (0, 2, 4, -2)


def place_of(first, g):
    return lanes() % 8 // 2 == (first + SHIFTS[g % 4]) % 8 // 2


def pack_sends(edges, to_east, to_west):
    for b in range(5):
        here = pl.ds(8 * b, 8)
        for first in range(0, GROUPS, 4):
            east, west = jnp.zeros((8, 128), f32), jnp.zeros((8, 128), f32)
            for g in range(first, min(first + 4, GROUPS)):
                value = roll(edges[g, here, :], SHIFTS[g % 4])
                east = jnp.where(place_of(2, g), value, east)
                west = jnp.where(place_of(4, g), value, west)
            to_east[first // 4, here, :] = east
            to_west[first // 4, here, :] = west


def unpack_sends(edges, left_in, right_in, halo):
    c = lanes() % 8 // 2
    for b in range(5):
        here = pl.ds(8 * b, 8)
        for g in range(GROUPS):
            mine = edges[g, here, :]
            halo[0, g, here, :] = jnp.where(c == 1, roll(left_in[g // 4, here, :], -SHIFTS[g % 4]), mine)
            halo[1, g, here, :] = jnp.where(c == 2, roll(right_in[g // 4, here, :], -SHIFTS[g % 4]), mine)


def pieces_kernel(currents, depth, slopes, offset, count, out, rows):
    me = lax.axis_index("ty") * 16 + lax.axis_index("tx")
    table = jnp.concatenate([currents[...], depth[...], slopes[...], jnp.zeros((3, 1024), f32)], 0)
    shifted = jnp.concatenate([roll(table, -s) for s in range(4)], 0)
    wanted = offset[pl.ds(me, 1), :]
    number = count[pl.ds(me, 1), :]
    chosen = (lax.broadcasted_iota(i32, (1024, 128), 0) == wanted).astype(f32).astype(bf16)
    picked = dot(split3(shifted), chosen)
    picked = picked[:32] + picked[32:64] + picked[64:]
    lane = lanes()
    for s in range(4):
        own = jnp.where(number > s, picked[8 * s : 8 * s + 8], 0.0)
        up, down = roll(own, -16), roll(own, 16)
        left = jnp.where(lane % 16 == 0, roll(own, -15), roll(own, 1))
        right = jnp.where(lane % 16 == 15, roll(own, 15), roll(own, -1))
        rows[pl.ds(16 * s, 16), :] = jnp.concatenate(
            [own[:5], up[1:3], down[1:3], left[0:1], left[2:3], right[0:1], right[2:3], jnp.zeros((3, 128), f32)], 0
        )
    rows[pl.ds(64, 64), :] = jnp.zeros((64, 128), f32)
    out[...] = jnp.transpose(rows[...])


def kinematics(water_depth, sigma):
    squared = sigma * sigma
    initial = squared / (gravity * jnp.sqrt(jnp.tanh(squared * water_depth / gravity)))
    hyperbolic = jnp.tanh(initial * water_depth)
    residue = gravity * initial * hyperbolic - squared
    derivative = gravity * hyperbolic + gravity * initial * water_depth * (1.0 - hyperbolic * hyperbolic)
    wavenumber = initial - residue / derivative
    product = jnp.minimum(wavenumber * water_depth, product_limit)
    growth = jnp.exp(2.0 * product)
    double = 0.5 * (growth - 1.0 / growth)
    return sigma / wavenumber * (0.5 + product / double), sigma / double


def pack_edges(rows):
    lane = lanes()
    total = jnp.zeros((8, 128), f32)
    for j, row in enumerate(rows):
        wide = jnp.broadcast_to(row, (8, 128))
        for at in range(8 * j, 128, 32):
            total = jnp.where((lane >= at) & (lane < at + 8), roll(wide, at + 4), total)
    return total


def faces(x, mask, axis):
    ahead = roll(x, -1, axis)
    value = (9.0 * (x + ahead) - roll(x, 1, axis) - roll(x, -2, axis)) * (0.5 / 16.0)
    return value * (mask * roll(mask, -1, axis))


def fields_kernel(
    arrived, count, sea, chip_in, z_in, left_in, right_in, sigma_rows, sigma_packed,
    cgx, cgy, tx, ty, ux, vy, water, edge_cg, edge_u,
):
    flip = parity()
    row, column = lax.axis_index("ty"), lax.axis_index("tx")
    up, down = row * 16 + column + 16, row * 16 + column - 16
    chip = jnp.where(flip == 1, down, up)
    beyond = jnp.where(flip == 1, up, down)
    left = row * 16 + lax.rem(column + 15, 16)
    right = row * 16 + lax.rem(column + 1, 16)
    tile = (row * 16 + column, chip, beyond, left, right)
    lane128 = lanes((128, 128))
    sub128 = lax.broadcasted_iota(i32, (128, 128), 0)
    select = jnp.zeros((128, 128), f32)
    for t in range(5):
        select = jnp.where((lane128 == t) & (sub128 == tile[t]), 1.0, select)
    columns = dot(count[...].astype(f32).astype(bf16), select.astype(bf16))
    below = (lane128 < sub128).astype(f32).astype(bf16)
    first = dot(below, columns.astype(bf16))

    masks = [
        sea[...].astype(f32),
        chip_in[0, pl.ds(BINS, 4), :],
        z_in[0, pl.ds(BINS, 4), :],
        left_in[0, pl.ds(40, 4), :],
        right_in[0, pl.ds(40, 4), :],
    ]
    stacked = jnp.concatenate(masks + [jnp.zeros((4, 128), f32)], 0)
    upto = (sub128 <= lane128).astype(f32).astype(bf16)
    prefix = dot(stacked.astype(bf16), upto)
    ranks = []
    for t in range(5):
        before = jnp.zeros((1, 1), f32)
        for r in range(4):
            line = prefix[4 * t + r : 4 * t + r + 1]
            ranks.append(jnp.where(masks[t][r : r + 1] > 0.5, line - 1.0 + before, -2.0))
            before = before + line[:, 127:128]

    def flipped(t, j, table):
        return jnp.where(flip == 1, table[4 * t + 3 - j], table[4 * t + j])

    mask_rows = [masks[t][r : r + 1] for t in range(5) for r in range(4)]
    own_rank = [flipped(0, j, ranks) for j in range(4)]
    own_mask = [flipped(0, j, mask_rows) for j in range(4)]
    chip_rank = [flipped(1, j, ranks) for j in range(2)]
    chip_mask = [flipped(1, j, mask_rows) for j in range(2)]
    z_rank = [flipped(2, 3 - j, ranks) for j in range(2)]
    z_mask = [flipped(2, 3 - j, mask_rows) for j in range(2)]
    left_rank = pack_edges([flipped(3, j, ranks) for j in range(4)])[0:1]
    right_rank = pack_edges([flipped(4, j, ranks) for j in range(4)])[0:1]
    left_mask = pack_edges([flipped(3, j, mask_rows) for j in range(4)])
    right_mask = pack_edges([flipped(4, j, mask_rows) for j in range(4)])

    turned = jnp.transpose(arrived[...])
    values = split3(jnp.concatenate([turned[16 * s : 16 * s + 16] for s in range(4)], 1))

    keys = []
    for t in range(5):
        number, start = columns[:, t : t + 1], first[:, t : t + 1]
        keys.append(
            jnp.concatenate([jnp.where(number > s, start + s, -1.0) for s in range(4)], 0)
        )

    def place(t, rank):
        chosen = (keys[t] == rank).astype(f32).astype(bf16)
        found = dot(values, chosen)
        return found[:16] + found[16:32] + found[32:]

    own = [place(0, own_rank[j]) for j in range(4)]
    near_chip = [place(1, chip_rank[j]) for j in range(2)]
    near_z = [place(2, z_rank[j]) for j in range(2)]
    found_left, found_right = place(3, left_rank), place(4, right_rank)

    def pick(found, chip_side, k):
        use_up = (flip == 0) if chip_side else (flip == 1)
        return jnp.where(use_up, found[5 + k : 6 + k], found[7 + k : 8 + k])

    def stack(rows):
        return jnp.concatenate(rows, 0)

    v8 = stack([pick(near_z[1], False, 0), pick(near_z[0], False, 0)] + [o[1:2] for o in own] + [pick(near_chip[0], True, 0), pick(near_chip[1], True, 0)])
    h8 = stack([pick(near_z[1], False, 1), pick(near_z[0], False, 1)] + [o[2:3] for o in own] + [pick(near_chip[0], True, 1), pick(near_chip[1], True, 1)])
    m8 = stack([z_mask[1], z_mask[0]] + own_mask + [chip_mask[0], chip_mask[1]])
    zero4 = jnp.zeros((4, 128), f32)
    own_m = stack(own_mask + [zero4])
    own_u = stack([o[0:1] for o in own] + [zero4])
    own_sx = stack([o[3:4] for o in own] + [zero4])
    own_sy = stack([o[4:5] for o in own] + [zero4])
    sign = jnp.where(flip == 1, -1.0, 1.0).astype(f32)
    water[...] = own_m
    depth8 = jnp.where(m8 > 0.5, h8, land_depth)
    m8s = m8 * courant_scale
    own_ms = own_m * courant_scale
    ux[...] = faces(own_u * own_ms, own_m, 1)
    vy[...] = roll(faces(v8 * m8s, m8, 0), -1, 0) * sign
    turn_x = own_sx * own_m * (0.5 * turn_scale)
    turn_y = own_sy * own_m * (0.5 * turn_scale)

    def one(f, carry):
        speed, turning = kinematics(depth8, jnp.broadcast_to(sigma_rows[pl.ds(f, 1), :], (8, 128)))
        cgy[f] = roll(faces(speed * m8s, m8, 0), -1, 0) * sign
        cgx[f] = faces(roll(speed, -2, 0) * own_ms, own_m, 1)
        turning = roll(turning, -2, 0)
        tx[f] = turning * turn_x
        ty[f] = turning * turn_y
        return carry

    lax.fori_loop(0, NF, one, 0, unroll=12)

    low = lanes() % 8 < 4
    own_mask_edge = pack_edges(own_mask)
    own_u_edge = pack_edges([o[0:1] for o in own])
    own_h_edge = pack_edges([o[2:3] for o in own])
    for side in range(2):
        outside = low if side == 0 else jnp.logical_not(low)
        found = found_left[9:11] if side == 0 else found_right[11:13]
        mask = jnp.where(outside, left_mask if side == 0 else right_mask, own_mask_edge)
        u = jnp.where(outside, found[0:1], own_u_edge)
        h = jnp.where(outside, found[1:2], own_h_edge)
        depth = jnp.where(mask > 0.5, h, land_depth)
        edge_u[side] = faces(u * (mask * courant_scale), mask, 1)
        for part in range(2):
            speed, _ = kinematics(depth, sigma_packed[pl.ds(8 * part, 8), :])
            edge_cg[side, pl.ds(8 * part, 8), :] = faces(speed * (mask * courant_scale), mask, 1)


def flux(speed, behind, ahead):
    return speed * jnp.where(speed > 0.0, behind, ahead)


def through_east(value, speed):
    triple = 3.0 * value
    return flux(speed, triple - roll(value, 1), roll(triple, -1) - roll(value, -2))


def step_kernel(high, make_fix, pack, last, again, halo, na, nb, *refs):
    refs = list(refs)
    take = lambda n: [refs.pop(0) for _ in range(n)]
    if make_fix:
        edges, left_in, right_in = take(3)
    else:
        (fix,) = take(1)
    cgx, cgy, tx, ty, ux, vy, water, edge_cg, edge_u, cosine, sine, stencil = take(12)
    other = take(1)[0] if pack or last else None
    if again:
        east_speed, north_speed, turn_speed = take(3)
    out = take(1)[0]
    if make_fix:
        (fix,) = take(1)
    if pack:
        out_edges, to_east, to_west = take(3)
    if not again:
        east_speed, north_speed, turn_speed = take(3)
    edge_halo, edge_flux, east, moved, turn, swirl, buffer, done = refs
    flip = parity()
    lane = lanes()
    low = lane % 8 < 4
    first = 2 if high else 0
    own = nb if high else na

    def edge_group(g, carry):
        for b, start in enumerate(STARTS):
            c = cosine[pl.ds(start, 8), :]
            for side in range(2):
                speed = c * edge_cg[side, pl.ds(g, 1), :] + edge_u[side]
                here = pl.ds(8 * b, 8)
                edge_flux[side, g, here, :] = through_east(edge_halo[side, g, here, :], speed)
        return carry

    def x_group(g, carry):
        places = [(q, start, j) for q in range(4) for start in STARTS for j in range(2)]
        value = jnp.concatenate([own[j, pl.ds((4 * g + q) * ND + start, 8), :] for q, start, j in places], 0)
        upper = value.astype(bf16)
        lower = (value - upper.astype(f32)).astype(bf16)
        sides = dot(jnp.concatenate([upper, lower], 1), stencil[...])
        for r, (q, start, j) in enumerate(places):
            f = 4 * g + q
            here = pl.ds(f * ND + start, 8)
            if again:
                speed = east_speed[j, here, :]
            else:
                c = cosine[pl.ds(start, 8), :]
                speed = c * cgx[f, pl.ds(first + j, 1), :] + ux[pl.ds(first + j, 1), :]
                east_speed[j, here, :] = speed
            both = sides[8 * r : 8 * r + 8]
            east[j, here, :] = flux(speed, both[:, :128], both[:, 128:])
        return carry

    def fix_group(g, carry):
        for b in range(5):
            here = pl.ds(8 * b, 8)
            left, right = edge_flux[0, g, here, :], edge_flux[1, g, here, :]
            fix[g, here, :] = jnp.where(low, right - roll(right, 1), left - roll(left, 1))
        return carry

    if make_fix:
        unpack_sends(edges, left_in, right_in, edge_halo)
        lax.fori_loop(0, GROUPS, edge_group, 0, unroll=3)
    x_group(0, 0)
    if make_fix:
        lax.fori_loop(0, GROUPS, fix_group, 0, unroll=9)
    at_edge = (lane < 2) | (lane >= 126)

    def one(g, q):
        f = 4 * g + q
        for b, start in enumerate(STARTS):
            base = f * ND + start
            c, s = cosine[pl.ds(start, 8), :], sine[pl.ds(start, 8), :]
            here = pl.ds(base, 8)
            value = [na[0, here, :], na[1, here, :], nb[0, here, :], nb[1, here, :]]
            if high:
                value = value + [halo[1, here, :], halo[0, here, :]]
            else:
                value = [halo[1, here, :], halo[0, here, :]] + value
            triple = [3.0 * v for v in value]
            across = []
            for k in range(3):
                if again:
                    speed = north_speed[k, here, :]
                else:
                    speed = s * cgy[f, pl.ds(first + k, 1), :] + vy[pl.ds(first + k, 1), :]
                    north_speed[k, here, :] = speed
                across.append(flux(speed, triple[k + 1] - value[k], triple[k + 2] - value[k + 3]))
            edge = fix[g, pl.ds(8 * b, 8), :]
            for j in range(2):
                row = first + j
                through = east[j, here, :]
                change = jnp.where(at_edge, roll(edge, -(32 * q + 8 * row + 4)), through - roll(through, 1))
                moved[q, j, pl.ds(8 + start, 8), :] = value[j + 2] - change - (across[j + 1] - across[j])
                if again:
                    continue
                half = s * tx[f, pl.ds(row, 1), :] - c * ty[f, pl.ds(row, 1), :]
                turn[q, j, pl.ds(8 + start, 8), :] = jnp.clip(half, -0.5 * refraction_limit, 0.5 * refraction_limit)
        for j in range(2):
            moved[q, j, pl.ds(8 + ND, 1), :] = moved[q, j, pl.ds(8, 1), :]
            if not again:
                turn[q, j, pl.ds(8 + ND, 1), :] = turn[q, j, pl.ds(8, 1), :]
            for start in STARTS:
                here = pl.ds((4 * g + q) * ND + start, 8)
                if again:
                    speed = turn_speed[j, here, :]
                else:
                    speed = turn[q, j, pl.ds(8 + start, 8), :] + turn[q, j, pl.ds(9 + start, 8), :]
                    turn_speed[j, here, :] = speed
                swirl[q, j, pl.ds(8 + start, 8), :] = flux(
                    speed, moved[q, j, pl.ds(8 + start, 8), :], moved[q, j, pl.ds(9 + start, 8), :]
                )
            swirl[q, j, pl.ds(7, 1), :] = swirl[q, j, pl.ds(7 + ND, 1), :]

    def finish(g, q, start):
        base = (4 * g + q) * ND + start
        for j in range(2):
            value = (
                moved[q, j, pl.ds(8 + start, 8), :]
                - swirl[q, j, pl.ds(8 + start, 8), :]
                + swirl[q, j, pl.ds(7 + start, 8), :]
            ) * water[pl.ds(first + j, 1), :]
            if last:
                buffer[pl.ds(4 * base + jnp.where(flip == 1, 3 - j, j), 8, stride=4), :] = value
                buffer[pl.ds(4 * base + jnp.where(flip == 1, 1 - j, 2 + j), 8, stride=4), :] = other[j, pl.ds(base, 8), :]
            else:
                out[j, pl.ds(base, 8), :] = value

    def result(g):
        rows = pl.ds(pl.multiple_of(576 * g, 8), 576)
        return pltpu.make_async_copy(buffer.at[rows, :], out.at[rows, :], done.at[g])

    def group(g, carry):
        for q in range(4):
            one(g, q)
        for q in range(4):
            for start in STARTS:
                finish(g, q, start)
        if last:
            result(g).start()
        x_group(jnp.minimum(g + 1, GROUPS - 1), 0)
        if pack:
            pack_group(other, out, out_edges, jnp.maximum(g - 1, 0))
        return carry

    lax.fori_loop(0, GROUPS, group, 0)
    if last:
        for g in range(GROUPS):
            result(g).wait()
    if pack:
        pack_group(other, out, out_edges, GROUPS - 1)
        pack_sends(out_edges, to_east, to_west)


def shape(*dims, dtype=f32):
    return jax.ShapeDtypeStruct(dims, dtype)


def call(kernel, out, scratch=(), limit=8, cost=2_000_000, moved=4_000_000, **specs):
    return pl.pallas_call(
        kernel,
        out_shape=out,
        scratch_shapes=list(scratch),
        compiler_params=pltpu.CompilerParams(vmem_limit_bytes=limit << 20),
        cost_estimate=pl.CostEstimate(flops=cost, bytes_accessed=moved, transcendentals=0),
        **specs,
    )


PLANE = shape(2, ROWS, 128)
EDGES = shape(GROUPS, 40, 128)
SENDS = shape(3, 48, 128)


def step(high, make_fix, pack, last, again, *operands):
    out = [shape(4 * BINS, 128) if last else PLANE]
    specs = {}
    if make_fix:
        out.append(shape(GROUPS, 40, 128))
    if pack:
        out += [EDGES, SENDS, SENDS]
    if not again:
        out += [shape(2, BINS, 128), shape(3, BINS, 128), shape(2, BINS, 128)]
    if last:
        specs["out_specs"] = [pl.BlockSpec(memory_space=pltpu.MemorySpace.HBM)]
    scratch = [
        pltpu.VMEM((2, GROUPS, 40, 128) if make_fix else (8, 128), f32),
        pltpu.VMEM((2, GROUPS, 40, 128) if make_fix else (8, 128), f32),
        pltpu.VMEM((2, BINS, 128), f32),
        pltpu.VMEM((4, 2, 56, 128), f32),
        pltpu.VMEM((4, 2, 56, 128), f32),
        pltpu.VMEM((4, 2, 56, 128), f32),
        pltpu.VMEM((4 * BINS + 32, 128) if last else (8, 128), f32),
        pltpu.SemaphoreType.DMA((GROUPS,)),
    ]
    return call(functools.partial(step_kernel, high, make_fix, pack, last, again), out, scratch, 8, **specs)(*operands)


Z_PAIRS = [p for z in range(3) for p in ((2 * z + 1, 2 * z + 2), (2 * z + 2, 2 * z + 1))]
CHIP_PAIRS = [p for z in range(4) for p in ((2 * z, 2 * z + 1), (2 * z + 1, 2 * z))]


def swap_z(rows):
    return lax.ppermute(rows, "ty", Z_PAIRS)


def swap_chip(rows):
    return lax.ppermute(rows, "ty", CHIP_PAIRS)


def swap_x(to_east, to_west):
    east = [(i, (i + 1) % 16) for i in range(16)]
    west = [((i + 1) % 16, i) for i in range(16)]
    return lax.ppermute(to_east, "tx", east), lax.ppermute(to_west, "tx", west)


def on_device(spectra, sea_mask, currents, sea_depth, slopes, piece_offset, piece_count):
    flat = spectra.reshape(4 * BINS, 128)
    hbm, vmem = (pl.BlockSpec(memory_space=kind) for kind in (pltpu.MemorySpace.HBM, pltpu.MemorySpace.VMEM))
    na, nb, edges, to_east, to_west, pieces = call(
        prepare_kernel,
        (PLANE, PLANE, EDGES, SENDS, SENDS, shape(128, 128)),
        [
            pltpu.VMEM((128, 128), f32),
            pltpu.VMEM((4 * BINS + 32, 128), f32),
            pltpu.VMEM(PLANE.shape, f32),
            pltpu.VMEM(PLANE.shape, f32),
            pltpu.SemaphoreType.DMA((GROUPS,)),
            pltpu.SemaphoreType.DMA((2, GROUPS + 1)),
        ],
        60,
        in_specs=[hbm] + [vmem] * 6,
        out_specs=[hbm] * 2 + [vmem] * 4,
    )(flat, sea_mask, currents, sea_depth.reshape(1, 1024), slopes, piece_offset, piece_count)
    z_in = swap_z(na)
    chip_in = swap_chip(nb)
    left_in, right_in = swap_x(to_east, to_west)
    arrived = lax.all_to_all(pieces, ("ty", "tx"), split_axis=0, concat_axis=0, tiled=True)
    per_frequency = shape(NF, 8, 128)
    speeds = call(
        fields_kernel, (per_frequency,) * 4 + (shape(8, 128),) * 3 + (shape(2, 16, 128), shape(2, 8, 128)), limit=12
    )(arrived, piece_count, sea_mask, chip_in, z_in, left_in, right_in, SIGMA_ROWS, SIGMA_PACKED)
    common = (*speeds, COSINE, SINE, STENCIL)
    new_a, fix, *low_speeds = step(False, True, False, False, False, z_in, na, nb, edges, left_in, right_in, *common)
    z_in = swap_z(new_a)
    new_b, edges, to_east, to_west, *high_speeds = step(True, False, True, False, False, chip_in, na, nb, fix, *common, new_a)
    chip_in = swap_chip(new_b)
    left_in, right_in = swap_x(to_east, to_west)
    end_b, fix = step(
        True, True, False, False, True, chip_in, new_a, new_b, edges, left_in, right_in, *common, *high_speeds
    )
    (out,) = step(False, False, False, True, True, z_in, new_a, new_b, fix, *common, end_b, *low_speeds)
    return out.reshape(spectra.shape)


def solution(mesh):
    return jax.shard_map(
        on_device,
        mesh=mesh,
        in_specs=(
            P(None, None, "ty", "tx"),
            P("ty", "tx"),
            P(None, ("ty", "tx")),
            P(("ty", "tx")),
            P(None, ("ty", "tx")),
            P(),
            P(),
        ),
        out_specs=P(None, None, "ty", "tx"),
        check_vma=False,
    )
```
